128 devices in a mesh: leaf: 128 (over z, y, x, core).
Axes of the slice: x: 4, y: 4, z: 4, core: 2. Of those that a mesh axis runs over, the one named last changes fastest.
Arguments:
- points: bfloat16 [262144, 128], P('leaf'), may hold values from -6 to 6
- charges: bfloat16 [262144, 256], P('leaf'), may hold values from -6 to 6
- order: int32 [128, 2048], P('leaf'), may hold values from 0 to 2047, each once within a row
- near: int32 [128, 2], P('leaf'), may hold values from 0 to 127, as said below
- bases: bfloat16 [262144, 256], P('leaf'), may hold values from -0.125 to 0.125
- lift_leaf: float32 [32768, 256], P('leaf'), may hold values from -0.1875 to 0.1875
- lift_node: float32 [8192, 256], P('leaf'), may hold values from -0.1875 to 0.1875
- proxy_leaf: float32 [32768, 128], P('leaf'), may hold values from -5 to 5
- proxy_node: float32 [8192, 128], P('leaf'), may hold values from -5 to 5
- proxy_top: float32 [2048, 128], P('leaf'), may hold values from -5 to 5
Outputs:
- potential: bfloat16 [262144, 256], P('leaf')
The draws below stay inside these ranges and needn't reach their ends.
Inputs may be any that keep to these rules, and one draw needn't show every extreme that they name: `order`: each row is a permutation of the leaf's 2048 positions. `near`: row l names two distinct leaves other than l from l's aligned group of four leaves; the relation is symmetric, and the group's remaining leaf is l's far partner, whose index differs from l in exactly one of the two lowest bits.
All inputs are finite; a program needn't handle non-finite values.
Results may differ from the reference program's by a relative error of at most 0.0049.
Values may be sent and summed in bfloat16 or wider, within the bound.
No kernel may reach another device: no remote copies, remote signals or barrier semaphores. Data moves between devices by JAX's collectives and lax.ppermute only.
A program may use at most 64 MiB of HBM per device.

```python
import jax
import jax.numpy as jnp
from jax import lax

D = 128
NRHS = 256
RANK = 256
LEAF = 2048
NPTS = 262144
TOPN = 8
N_LEAF = 128


def draw_near(key, part):
    drawn_bits = jax.random.randint(key, (N_LEAF // 4,), 1, 3)
    group_ids = jnp.arange(N_LEAF // 4, dtype=jnp.int32)
    partner_bits = jnp.where(group_ids % 2 == 0, 2, drawn_bits).astype(jnp.int32)
    leaf_ids = jnp.arange(N_LEAF, dtype=jnp.int32)
    leaf_slot = leaf_ids % 4
    spread = jnp.repeat(partner_bits, 4).astype(jnp.int32)
    first_bits = jnp.where(spread == 1, 2, 1).astype(jnp.int32)
    second_bits = jnp.full((N_LEAF,), 3, jnp.int32)
    start = leaf_ids - leaf_slot
    first_near = start + jnp.bitwise_xor(leaf_slot, first_bits)
    second_near = start + jnp.bitwise_xor(leaf_slot, second_bits)
    return jnp.stack([first_near, second_near], axis=1).astype(jnp.int32)


def level_offset(key, salt):
    offset_key = jax.random.fold_in(key, salt)
    sign_key, size_key = jax.random.split(offset_key)
    signs = jnp.where(jax.random.bernoulli(sign_key, 0.5, (D,)), 1.0, -1.0).astype(jnp.float32)
    sizes = jax.random.uniform(size_key, (D,), jnp.float32, 0.45, 0.75)
    return signs * sizes


def normal_proxy(key, rows, salt):
    offset = level_offset(key, salt)
    noise = 0.75 * jax.random.normal(jax.random.fold_in(key, salt + 1), (rows, D), jnp.float32)
    return jnp.clip(offset[None, :] + noise, -5.0, 5.0).astype(jnp.float32)


def draw_proxy_leaf(key, part):
    return normal_proxy(key, N_LEAF * RANK, 101)


def draw_proxy_node(key, part):
    return normal_proxy(key, N_LEAF // 4 * RANK, 203)


def draw_proxy_top(key, part):
    return normal_proxy(key, TOPN * RANK, 307)


def steps_of(stream_key, dims, cuts, low, largest):
    loudness, own = 1.0, jax.random.fold_in(stream_key, 6)
    for dim, blocks in cuts:
        draws = jnp.exp(jax.random.uniform(jax.random.fold_in(own, dim), (blocks,), jnp.float32, low / len(cuts), largest / len(cuts)))
        loudness = loudness * jnp.repeat(draws, dims[dim] // blocks).reshape([-1 if axis == dim else 1 for axis in range(len(dims))])
    return loudness


def centred(key, shape, scale, most, cuts=(), held_as=jnp.bfloat16):
    values = scale * jax.random.normal(key, shape, jnp.float32)
    if cuts:
        values = values * steps_of(key, shape, cuts, -0.22, 0.18)
    return jnp.clip(values, -most, most).astype(held_as)


def setup_inputs(seed: int = 0) -> dict:
    streams_of = jax.random.split(jax.random.key(seed), 11)
    return {
        "points": centred(streams_of[0], (NPTS, D), 1.0, 6.0, ((0, 128),)),
        "charges": centred(streams_of[1], (NPTS, NRHS), 1.0, 6.0, ((0, 128),)),
        "order": jax.vmap(lambda own: jax.random.permutation(own, LEAF))(jax.random.split(streams_of[2], N_LEAF)).reshape((N_LEAF, LEAF)).astype(jnp.int32),
        "near": draw_near(jax.random.fold_in(streams_of[10], 71), 0),
        "bases": centred(streams_of[4], (NPTS, RANK), LEAF ** -0.5, 0.125, ((0, 128),)),
        "lift_leaf": centred(streams_of[5], (N_LEAF * RANK, RANK), (4 * RANK) ** -0.5, 0.1875, ((0, 128),), jnp.float32),
        "lift_node": centred(streams_of[6], (N_LEAF // 4 * RANK, RANK), (4 * RANK) ** -0.5, 0.1875, ((0, 128),), jnp.float32),
        "proxy_leaf": draw_proxy_leaf(jax.random.fold_in(streams_of[10], 71), 0),
        "proxy_node": draw_proxy_node(jax.random.fold_in(streams_of[10], 71), 0),
        "proxy_top": draw_proxy_top(jax.random.fold_in(streams_of[10], 71), 0),
    }


highest = lax.Precision.HIGHEST


def kernel_tile(left, right):
    products = jnp.dot(left, right.T, preferred_element_type=jnp.float32)
    left_norm = jnp.sum(jnp.square(left.astype(jnp.float32)), axis=1)
    right_norm = jnp.sum(jnp.square(right.astype(jnp.float32)), axis=1)
    return jnp.exp((2.0 * products - left_norm[:, None] - right_norm[None, :]) * (2.0 / D))


def couple(left, right):
    products = jnp.dot(left, right.T, precision=highest)
    left_norm = jnp.sum(left * left, axis=1)
    right_norm = jnp.sum(right * right, axis=1)
    return jnp.exp((2.0 * products - left_norm[:, None] - right_norm[None, :]) * (2.0 / D))


def reference(points, charges, order, near, bases, lift_leaf, lift_node, proxy_leaf, proxy_node, proxy_top):
    leaf_points = points.reshape(N_LEAF, LEAF, D)
    leaf_rhs = jnp.take_along_axis(charges.reshape(N_LEAF, LEAF, NRHS), order[:, :, None], axis=1)
    leaf_bases = bases.reshape(N_LEAF, LEAF, RANK)

    def near_leaf(leaf_id):
        total = jnp.zeros((LEAF, NRHS), jnp.float32)
        own = leaf_points[leaf_id]
        for source in (leaf_id, near[leaf_id, 0], near[leaf_id, 1]):
            tile = kernel_tile(own, leaf_points[source]).astype(jnp.bfloat16)
            total = total + jnp.dot(tile, leaf_rhs[source], preferred_element_type=jnp.float32)
        return total

    near_sum = lax.map(near_leaf, jnp.arange(N_LEAF, dtype=jnp.int32))

    def leaf_coeff(pair):
        return lax.dot_general(pair[0], pair[1], (((0,), (0,)), ((), ())), preferred_element_type=jnp.float32)

    coefficient = lax.map(leaf_coeff, (leaf_bases, leaf_rhs))
    lifts = lift_leaf.reshape(N_LEAF, RANK, RANK)
    upward = jnp.einsum("lkr,lkc->lrc", lifts, coefficient, precision=highest)
    node_coeff = upward.reshape(N_LEAF // 4, 4, RANK, NRHS).sum(axis=1)
    node_lifts = lift_node.reshape(N_LEAF // 4, RANK, RANK)
    top_coeff = jnp.einsum("gkr,gkc->grc", node_lifts, node_coeff, precision=highest)
    top_coeff = top_coeff.reshape(TOPN, 4, RANK, NRHS).sum(axis=1)
    leaf_proxy = proxy_leaf.reshape(N_LEAF, RANK, D)
    node_proxy = proxy_node.reshape(N_LEAF // 4, RANK, D)
    top_flat = top_coeff.reshape(TOPN * RANK, NRHS)
    owner = jnp.arange(TOPN * RANK, dtype=jnp.int32) // RANK

    def top_field(node):
        kernel = couple(lax.dynamic_slice_in_dim(proxy_top, node * RANK, RANK, 0), proxy_top)
        kernel = jnp.where(owner[None, :] != node, kernel, 0.0)
        return jnp.dot(kernel, top_flat, precision=highest)

    field_top = lax.map(top_field, jnp.arange(TOPN, dtype=jnp.int32))
    group_proxy = node_proxy.reshape(N_LEAF // 16, 4 * RANK, D)
    group_coeff = node_coeff.reshape(N_LEAF // 16, 4 * RANK, NRHS)
    sibling_owner = jnp.arange(4 * RANK, dtype=jnp.int32) // RANK

    def node_field(node):
        kernel = couple(node_proxy[node], group_proxy[node // 4])
        kernel = jnp.where(sibling_owner[None, :] != node % 4, kernel, 0.0)
        far_part = jnp.dot(kernel, group_coeff[node // 4], precision=highest)
        return far_part + jnp.dot(node_lifts[node], field_top[node // 4], precision=highest)

    field_node = lax.map(node_field, jnp.arange(N_LEAF // 4, dtype=jnp.int32))
    group_leaf_proxy = leaf_proxy.reshape(N_LEAF // 4, 4 * RANK, D)
    group_leaf_coeff = coefficient.reshape(N_LEAF // 4, 4 * RANK, NRHS)

    def leaf_field(leaf_id):
        partner = 6 - leaf_id % 4 - near[leaf_id, 0] % 4 - near[leaf_id, 1] % 4
        kernel = couple(leaf_proxy[leaf_id], group_leaf_proxy[leaf_id // 4])
        kernel = jnp.where(sibling_owner[None, :] == partner, kernel, 0.0)
        far_part = jnp.dot(kernel, group_leaf_coeff[leaf_id // 4], precision=highest)
        far_part = far_part + jnp.dot(lifts[leaf_id], field_node[leaf_id // 4], precision=highest)
        return far_part.astype(jnp.bfloat16)

    field_leaf = lax.map(leaf_field, jnp.arange(N_LEAF, dtype=jnp.int32))

    def descend(pair):
        return jnp.dot(pair[0], pair[1], preferred_element_type=jnp.float32)

    descent = lax.map(descend, (leaf_bases, field_leaf))
    return (near_sum + descent).astype(jnp.bfloat16).reshape(N_LEAF * LEAF, NRHS)
```

```python
import functools

import jax
import jax.numpy as jnp
from jax import lax
from jax.experimental import pallas as pl
from jax.experimental.pallas import tpu as pltpu
from jax.sharding import PartitionSpec as P

D = 128
NRHS = 256
RANK = 256
LEAF = 2048
AXIS = "leaf"
BF = jnp.bfloat16
F32 = jnp.float32
SCALE = 4.0 / D * 1.4426950408889634
CHUNKS = ((0, 1024), (1024, 1024))


def dot(a, b):
    return lax.dot_general(a, b, (((1,), (0,)), ((), ())), preferred_element_type=F32)


def dot_t(a, b):
    return lax.dot_general(a, b, (((1,), (1,)), ((), ())), preferred_element_type=F32)


def widened(x, left):
    wide = x.astype(F32)
    rest = 0.5 * jnp.sum(wide * wide, axis=1, keepdims=True)
    high = rest.astype(BF).astype(F32)
    rest = rest - high
    middle = rest.astype(BF).astype(F32)
    low = rest - middle
    lane = lax.broadcasted_iota(jnp.int32, (x.shape[0], 128), 1)
    first, ones = (0, 3) if left else (3, 0)
    extra = jnp.where(
        lane == first, -high, jnp.where(lane == first + 1, -middle, jnp.where(lane == first + 2, -low, 0.0))
    )
    extra = jnp.where((lane >= ones) & (lane < ones + 3), 1.0, extra)
    return jnp.concatenate([x.astype(BF), extra.astype(BF)], axis=1)


def gauss(left, right):
    return jnp.exp2(dot_t(left, right) * SCALE).astype(BF)


def call(body, outs, *args, name, scratch=(), smem=0, flops=0, aliases=None):
    specs = [
        pl.BlockSpec(memory_space=pltpu.SMEM if i < smem else pltpu.VMEM) for i in range(len(args))
    ]
    return pl.pallas_call(
        body,
        out_shape=[jax.ShapeDtypeStruct(s, d) for s, d in outs],
        in_specs=specs,
        out_specs=[pl.BlockSpec(memory_space=pltpu.VMEM)] * len(outs),
        scratch_shapes=list(scratch),
        input_output_aliases=aliases or {},
        name=name,
        cost_estimate=pl.CostEstimate(flops=flops, bytes_accessed=1 << 20, transcendentals=0),
        compiler_params=pltpu.CompilerParams(vmem_limit_bytes=44 << 20),
    )(*args)


def prep_body(meta, order, points, charges, bases, lift, proxy, own_w, rhs, far, keep, send, up):
    core = meta[0]
    own_w[...] = widened(points[...], True)
    tall = jnp.concatenate([order[...].astype(F32)] * 8, axis=0).T
    places = lax.broadcasted_iota(jnp.int32, (128, LEAF), 1).astype(F32)
    for b in range(LEAF // 128):
        hot = jnp.where(tall[:, b : b + 1] == places, 1.0, 0.0).astype(BF)
        rhs[b * 128 : (b + 1) * 128, :] = dot(hot, charges[...]).astype(BF)
    coef = lax.dot_general(rhs[...], bases[...], (((0,), (0,)), ((), ())), preferred_element_type=F32)
    coef = coef.astype(BF)
    far[0:RANK, :] = coef
    far[RANK:, 0:D] = proxy[0:128, :].astype(BF)
    far[RANK:, D:] = proxy[128:256, :].astype(BF)
    up[...] = dot(coef, lift[...].astype(BF))
    keep[...] = up[pl.ds(pl.multiple_of(core * 128, 128), 128), :]
    send[...] = up[pl.ds(pl.multiple_of((1 - core) * 128, 128), 128), :].astype(BF)


def halve_body(meta, keep, got, kept, send, total):
    u = meta[1]
    total[...] = keep[...] + got[...].astype(F32)
    kept[...] = total[pl.ds(pl.multiple_of(u * 64, 64), 64), :]
    send[...] = total[pl.ds(pl.multiple_of((1 - u) * 64, 64), 64), :].astype(BF)


def node_body(meta, kept, got, stat, send, lift):
    slot = meta[3]
    for j in range(4):
        at = pl.multiple_of((slot ^ j) * 64, 64)
        lift[pl.ds(at, 64), 0:128] = stat[j, 0:64, :]
        lift[pl.ds(at, 64), 128:256] = stat[j, 64:128, :]
    node = (kept[...] + got[...].astype(F32)).astype(BF)
    send[0:64, :] = node
    send[64:128, :] = dot(node, lift[...]).astype(BF)


def pair_body(mine, got, send):
    send[0:64, :] = mine[0:64, :]
    send[64:128, :] = got[0:64, :]
    send[128:192, :] = (mine[64:128, :].astype(F32) + got[64:128, :].astype(F32)).astype(BF)


def coupling_body(meta, nodes, tops, kernel_one, kernel_two, z_node, z_top):
    slot, part = meta[3], meta[4]
    for h in range(4):
        for j in range(4):
            at = (slot ^ (2 * (h % 2)) ^ j) * 64
            z_node[pl.ds(pl.multiple_of(h * 256 + at, 64), 64), :] = nodes[4 * h + j, 0:64, :]
    for r in range(8):
        for k in range(16):
            place = (k & 1) ^ (k & 2) ^ (6 * (k // 4 % 2)) ^ (8 * (k // 8)) ^ (8 * (r % 2))
            at = (part ^ place) * 16
            z_top[pl.ds(pl.multiple_of(r * 256 + at, 16), 16), :] = tops[16 * r + k, :, :]
    own = widened(z_node[0:256, :], False)
    for h in range(1, 4):
        kernel_one[(h - 1) * 256 : h * 256, :] = gauss(widened(z_node[h * 256 : (h + 1) * 256, :], True), own)
    own = widened(z_top[0:256, :], False)
    for r in range(1, 8):
        kernel_two[(r - 1) * 256 : r * 256, :] = gauss(widened(z_top[r * 256 : (r + 1) * 256, :], True), own)


def field_body(sibs_a, sibs_b, low, high, kernel_one, kernel_two, lift, out):
    field = dot(low[64:128, :], kernel_two[0:256, :])
    for r in range(2, 8):
        part = low[r * 64 : (r + 1) * 64, :] if r < 4 else high[(r - 4) * 64 : (r - 3) * 64, :]
        field += dot(part, kernel_two[(r - 1) * 256 : r * 256, :])
    total = dot_t(field.astype(BF), lift[...])
    total += dot(sibs_a[64:128, :], kernel_one[0:256, :])
    total += dot(sibs_b[0:64, :], kernel_one[256:512, :])
    total += dot(sibs_b[64:128, :], kernel_one[512:768, :])
    out[...] = total.astype(BF)


def join_body(meta, mine, got, out):
    u = meta[1]
    out[pl.ds(pl.multiple_of(u * 64, 64), 64), :] = mine[...]
    out[pl.ds(pl.multiple_of((1 - u) * 64, 64), 64), :] = got[...]


def near_tile(own_w, other_w, values, acc, first, rows, block=512):
    for r in range(0, rows, block):
        total = None if first else acc[r : r + block, :]
        for c in range(0, other_w.shape[0], 256):
            tile = gauss(own_w[r : r + block, :], other_w[c : c + 256, :])
            part = dot(tile, values[c : c + 256, :])
            total = part if total is None else total + part
        acc[r : r + block, :] = total


def own_body(own_w, points, rhs, acc, other_w):
    other_w[...] = widened(points[...], False)
    near_tile(own_w, other_w, rhs, acc, True, own_w.shape[0])


def chunk_body(own_w, pts_a, rhs_a, pts_b, rhs_b, acc_in, acc, other_w):
    n = rhs_a.shape[0]
    other_w[0:n, :] = widened(pts_a[...], False)
    other_w[n:, :] = widened(pts_b[...], False)
    for r in range(0, LEAF, 512):
        total = acc_in[r : r + 512, :]
        for values, base in ((rhs_a, 0), (rhs_b, n)):
            for c in range(0, n, 256):
                tile = gauss(own_w[r : r + 512, :], other_w[base + c : base + c + 256, :])
                total += dot(tile, values[c : c + 256, :])
        acc[r : r + 512, :] = total


def last_body(
    meta, own_w, pts_a, rhs_a, pts_b, rhs_b, acc_in, bases, far_one, far_two, proxy, lift, half, got,
    out, other_w, far, node,
):
    n = rhs_a.shape[0]
    core = meta[0]

    @pl.when(meta[2] == 1)
    def _():
        far[...] = far_one[...]

    @pl.when(meta[2] == 0)
    def _():
        far[...] = far_two[...]

    z_far = jnp.concatenate([far[RANK:, 0:D], far[RANK:, D:]], axis=0)
    kernel = gauss(widened(z_far, True), widened(proxy[...].astype(BF), False))
    node[pl.ds(pl.multiple_of(core * 128, 128), 128), :] = half[...]
    node[pl.ds(pl.multiple_of((1 - core) * 128, 128), 128), :] = got[...]
    field = dot(far[0:RANK, :], kernel) + dot_t(node[...], lift[...].astype(BF))
    field = field.astype(BF)
    other_w[0:n, :] = widened(pts_a[...], False)
    other_w[n:, :] = widened(pts_b[...], False)
    for r in range(0, LEAF, 512):
        total = acc_in[r : r + 512, :] + dot_t(bases[r : r + 512, :], field)
        for values, base in ((rhs_a, 0), (rhs_b, n)):
            for c in range(0, n, 256):
                tile = gauss(own_w[r : r + 512, :], other_w[base + c : base + c + 256, :])
                total += dot(tile, values[c : c + 256, :])
        out[r : r + 512, :] = total.astype(BF)


def swap(x, flip):
    n = lax.axis_size(AXIS)
    return lax.ppermute(x, AXIS, [(i, i ^ flip) for i in range(n)])


def per_device(
    points, charges, order, near, bases, lift_leaf, lift_node, proxy_leaf, proxy_node, proxy_top
):
    me = lax.axis_index(AXIS)
    slot = me % 4
    x = me // 2 % 4
    far_flip = (6 - slot - near[0, 0] % 4 - near[0, 1] % 4) ^ slot
    far_core = (far_flip == 1).astype(jnp.int32)
    meta = jnp.stack([me % 2, (x % 2) ^ (x // 2), far_core, slot, me % 16]).astype(jnp.int32)

    lift_rows = lift_node.astype(BF)
    zn, zt = proxy_node.astype(BF), proxy_top.astype(BF)
    stat = jnp.concatenate([lift_rows[:, :128], lift_rows[:, 128:], zn, zt], axis=0)[None]
    stat = jnp.concatenate([stat, swap(stat, 1)], axis=0)
    stat = jnp.concatenate([stat, swap(stat, 2)], axis=0)
    own_z = stat[:, 128:]
    own_z = jnp.concatenate([own_z, swap(own_z, 6)], axis=0)
    own_z = jnp.concatenate([own_z, swap(own_z, 8)], axis=0)
    nodes, tops = own_z[:, :64], own_z[:, 64:]
    for flip in (24, 32, 96):
        tops = jnp.concatenate([tops, swap(tops, flip)], axis=0)
    kernel_one, kernel_two = call(
        coupling_body, [((768, 256), BF), ((1792, 256), BF)], meta, nodes, tops,
        name="coupling", smem=1, flops=1 << 30,
        scratch=[pltpu.VMEM((1024, 128), BF), pltpu.VMEM((2048, 128), BF)],
    )

    pts_a = swap(points, 3)
    own_w, rhs, far_out, keep, send = call(
        prep_body,
        [((LEAF, 256), BF), ((LEAF, NRHS), BF), ((384, 256), BF), ((128, 256), F32), ((128, 256), BF)],
        meta, order.reshape(16, 128), points, charges, bases, lift_leaf, proxy_leaf,
        name="prep", smem=1, flops=5 << 30, scratch=[pltpu.VMEM((256, 256), F32)],
    )

    kept, send = call(
        halve_body, [((64, 256), F32), ((64, 256), BF)], meta, keep, swap(send, 1),
        name="halve", smem=1, scratch=[pltpu.VMEM((128, 256), F32)],
    )
    send_three, lift_all = call(
        node_body, [((128, 256), BF), ((256, 256), BF)], meta, kept, swap(send, 2), stat,
        name="node", smem=1,
    )
    send_four, = call(pair_body, [((192, 256), BF)], send_three, swap(send_three, 6), name="pair")
    got_four = swap(send_four, 8)
    top = (send_four[128:].astype(F32) + got_four[128:].astype(F32)).astype(BF)
    low = jnp.concatenate([top, swap(top, 24)], axis=0)
    low = jnp.concatenate([low, swap(low, 32)], axis=0)
    high = swap(low, 96)
    quarter, = call(
        field_body, [((64, 256), BF)], send_four, got_four, low, high, kernel_one, kernel_two, lift_all,
        name="field", flops=1 << 29,
    )
    half, = call(join_body, [((128, 256), BF)], meta, quarter, swap(quarter, 2), name="join", smem=1)
    other_half = swap(half, 1)

    chosen = jnp.where(far_core == 1, pts_a, points)
    pts_b = swap(chosen, 1)
    rhs_a = [swap(rhs[s : s + n], 3) for s, n in CHUNKS]
    rhs_b = [swap(jnp.where(far_core == 1, got, rhs[s : s + n]), 1) for got, (s, n) in zip(rhs_a, CHUNKS)]
    far_one, far_two = swap(far_out, 1), swap(far_out, 2)
    acc, = call(
        own_body, [((LEAF, NRHS), F32)], own_w, points, rhs, name="near_own", flops=6 << 30,
        scratch=[pltpu.VMEM((LEAF, 256), BF)],
    )
    (s, n) = CHUNKS[0]
    acc, = call(
        chunk_body, [((LEAF, NRHS), F32)], own_w, pts_a[s : s + n], rhs_a[0], pts_b[s : s + n], rhs_b[0], acc,
        name="near_chunk", flops=6 << 30, scratch=[pltpu.VMEM((2 * n, 256), BF)], aliases={5: 0},
    )
    (s, n) = CHUNKS[1]
    out, = call(
        last_body, [((LEAF, NRHS), BF)],
        meta, own_w, pts_a[s : s + n], rhs_a[1], pts_b[s : s + n], rhs_b[1], acc, bases, far_one, far_two,
        proxy_leaf, lift_leaf, half, other_half,
        name="near_last", smem=1, flops=6 << 30,
        scratch=[pltpu.VMEM((2 * n, 256), BF), pltpu.VMEM((384, 256), BF), pltpu.VMEM((256, 256), BF)],
    )
    return out


def solution(mesh):
    spec = P(AXIS, None)
    return jax.shard_map(
        per_device, mesh=mesh, in_specs=(spec,) * 10, out_specs=spec, check_vma=False
    )
```

```python
import functools

import jax
import jax.numpy as jnp
from jax import lax
from jax.experimental import pallas as pl
from jax.experimental.pallas import tpu as pltpu
from jax.sharding import PartitionSpec as P

D = 128
NRHS = 256
RANK = 256
LEAF = 2048
AXIS = "leaf"
BF = jnp.bfloat16
F32 = jnp.float32
SCALE = 4.0 / D * 1.4426950408889634
FAR = 384
CHUNKS = ((0, 512), (512, 512), (1024, 512), (1536, 512))
BASES = (0, FAR, 0, 0)
HALF = LEAF // 2


def dot(a, b):
    return lax.dot_general(a, b, (((1,), (0,)), ((), ())), preferred_element_type=F32)


def dot_t(a, b):
    return lax.dot_general(a, b, (((1,), (1,)), ((), ())), preferred_element_type=F32)


def widened(x, left):
    wide = x.astype(F32)
    rest = 0.5 * jnp.sum(wide * wide, axis=1, keepdims=True)
    high = rest.astype(BF).astype(F32)
    rest = rest - high
    middle = rest.astype(BF).astype(F32)
    low = rest - middle
    lane = lax.broadcasted_iota(jnp.int32, (x.shape[0], 128), 1)
    first, ones = (0, 3) if left else (3, 0)
    extra = jnp.where(
        lane == first, -high, jnp.where(lane == first + 1, -middle, jnp.where(lane == first + 2, -low, 0.0))
    )
    extra = jnp.where((lane >= ones) & (lane < ones + 3), 1.0, extra)
    return jnp.concatenate([x.astype(BF), extra.astype(BF)], axis=1)


def gauss(left, right):
    return jnp.exp2(dot_t(left, right) * SCALE).astype(BF)


def call(body, outs, *args, name, scratch=(), smem=0, hbm=(), aliases=None, limit=24):
    def space(i):
        return pltpu.SMEM if i < smem else pltpu.HBM if i in hbm else pltpu.VMEM

    args = [
        pltpu.with_memory_space_constraint(arg, pltpu.HBM) if i in hbm else arg for i, arg in enumerate(args)
    ]
    return pl.pallas_call(
        body,
        out_shape=[jax.ShapeDtypeStruct(s, d) for s, d in outs],
        in_specs=[pl.BlockSpec(memory_space=space(i)) for i in range(len(args))],
        out_specs=[pl.BlockSpec(memory_space=pltpu.VMEM)] * len(outs),
        scratch_shapes=list(scratch),
        input_output_aliases=aliases or {},
        name=name,
        cost_estimate=pl.CostEstimate(flops=0, bytes_accessed=0, transcendentals=0),
        compiler_params=pltpu.CompilerParams(vmem_limit_bytes=limit << 20),
    )(*args)


def place():
    me = lax.axis_index(AXIS)
    x = lax.rem(lax.div(me, 2), 4)
    return lax.rem(me, 2), lax.rem(x, 2) ^ lax.div(x, 2), lax.rem(me, 4), lax.rem(me, 16)


def far_is_core(near):
    slot = place()[2]
    return ((6 - slot - lax.rem(near[0, 0], 4) - lax.rem(near[0, 1], 4)) ^ slot) == 1


def choose_body(skip, near, got, own, out):
    core = far_is_core(near)

    @pl.when(core)
    def _():
        out[skip:, :] = got[skip:, :]
        if skip:
            out[0:skip, :] = own[0:skip, :]

    @pl.when(jnp.logical_not(core))
    def _():
        out[skip:, :] = own[skip:, :]
        if skip:
            out[0:skip, :] = got[0:skip, :]


def fetched(pairs, sems):
    copies = [pltpu.make_async_copy(src, dst, sems.at[i]) for i, (src, dst) in enumerate(pairs)]
    for copy in copies:
        copy.start()
    return copies


def pack_body(lift_h, node_h, top_h, out, lift, node, top, sems):
    for copy in fetched(((lift_h, lift), (node_h, node), (top_h, top)), sems):
        copy.wait()
    out[0:64, :] = lift[:, 0:128].astype(BF)
    out[64:128, :] = lift[:, 128:256].astype(BF)
    out[128:192, :] = node[...].astype(BF)
    out[192:208, :] = top[...].astype(BF)


def cat_body(one, two, out):
    n = one.shape[0]
    out[0:n] = one[...]
    out[n:] = two[...]


def cat_z_body(a, b, c, d, out):
    for j, stat in enumerate((a, b, c, d)):
        out[j] = stat[128:, :]


def tops_body(z_a, z_b, out):
    out[0:8] = z_a[:, 64:, :]
    out[8:16] = z_b[:, 64:, :]


def prep_body(
    order, points_h, charges_h, bases_h, lift_h, proxy_h,
    own_l, own_r, buf_zero, buf_one, buf_two, buf_three, keep, send,
    points, charges, bases, lift, proxy, up, sems,
):
    core = place()[0]
    pairs = ((charges_h, charges), (points_h, points), (bases_h, bases), (lift_h, lift), (proxy_h, proxy))
    copies = fetched(pairs, sems)
    rows = [order[:, b * 128 : (b + 1) * 128] for b in range(LEAF // 128)]
    tall = jnp.concatenate(rows * (128 // len(rows)), axis=0).astype(F32).T
    places = lax.broadcasted_iota(jnp.int32, (128, LEAF), 1).astype(F32)
    copies[0].wait()
    coef = None
    for i, (buf, (start, n)) in enumerate(zip((buf_zero, buf_one, buf_two, buf_three), CHUNKS)):
        base = BASES[i]
        for b in range(n // 128):
            at = start // 128 + b
            hot = jnp.where(tall[:, at : at + 1] == places, 1.0, 0.0).astype(BF)
            buf[base + b * 128 : base + (b + 1) * 128, :] = dot(hot, charges[...]).astype(BF)
        if i == 0:
            copies[1].wait()
            copies[2].wait()
        part = lax.dot_general(
            buf[base : base + n, :], bases[start : start + n, :], (((0,), (0,)), ((), ())),
            preferred_element_type=F32,
        )
        coef = part if coef is None else coef + part
    copies[3].wait()
    copies[4].wait()
    coef = coef.astype(BF)
    buf_one[0:RANK, :] = coef
    buf_one[RANK:FAR, 0:D] = proxy[0:128, :].astype(BF)
    buf_one[RANK:FAR, D:] = proxy[128:256, :].astype(BF)
    up[...] = dot(coef, lift[...].astype(BF))
    keep[...] = up[pl.ds(pl.multiple_of(core * 128, 128), 128), :]
    send[...] = up[pl.ds(pl.multiple_of((1 - core) * 128, 128), 128), :].astype(BF)
    own_l[...] = widened(points[...], True)
    own_r[...] = widened(points[...], False)


def halve_body(keep, got, kept, send, total):
    u = place()[1]
    total[...] = keep[...] + got[...].astype(F32)
    kept[...] = total[pl.ds(pl.multiple_of(u * 64, 64), 64), :]
    send[...] = total[pl.ds(pl.multiple_of((1 - u) * 64, 64), 64), :].astype(BF)


def node_body(kept, got, stat_a, stat_b, stat_c, stat_d, send, lift):
    slot = place()[2]
    for j, stat in enumerate((stat_a, stat_b, stat_c, stat_d)):
        at = pl.multiple_of((slot ^ j) * 64, 64)
        lift[pl.ds(at, 64), 0:128] = stat[0:64, :]
        lift[pl.ds(at, 64), 128:256] = stat[64:128, :]
    node = (kept[...] + got[...].astype(F32)).astype(BF)
    send[0:64, :] = node
    send[64:128, :] = dot(node, lift[...]).astype(BF)


def pair_body(mine, got, send):
    send[0:64, :] = mine[0:64, :]
    send[64:128, :] = got[0:64, :]
    send[128:192, :] = (mine[64:128, :].astype(F32) + got[64:128, :].astype(F32)).astype(BF)


def top_body(mine, got, out):
    out[...] = (mine[128:192, :].astype(F32) + got[128:192, :].astype(F32)).astype(BF)


def node_coupling_body(nodes_a, nodes_b, out, z_node):
    slot = place()[2]
    for h in range(4):
        nodes = nodes_a if h < 2 else nodes_b
        for j in range(4):
            at = (slot ^ (2 * (h % 2)) ^ j) * 64
            z_node[pl.ds(pl.multiple_of(h * 256 + at, 64), 64), :] = nodes[4 * (h % 2) + j, 0:64, :]
    own = widened(z_node[0:256, :], False)
    for h in range(1, 4):
        out[(h - 1) * 256 : h * 256, :] = gauss(widened(z_node[h * 256 : (h + 1) * 256, :], True), own)


def top_coupling_body(tops_a, tops_b, out, z_top):
    part = place()[3]
    for r in range(8):
        tops = tops_a if r < 4 else tops_b
        for k in range(16):
            offset = (k & 1) ^ (k & 2) ^ (6 * (k // 4 % 2)) ^ (8 * (k // 8)) ^ (8 * (r % 2))
            at = (part ^ offset) * 16
            z_top[pl.ds(pl.multiple_of(r * 256 + at, 16), 16), :] = tops[16 * (r % 4) + k, :, :]
    own = widened(z_top[0:256, :], False)
    for r in range(1, 8):
        out[(r - 1) * 256 : r * 256, :] = gauss(widened(z_top[r * 256 : (r + 1) * 256, :], True), own)


def field_body(sibs_a, sibs_b, low, high, kernel_one, kernel_two, lift, out):
    field = dot(low[64:128, :], kernel_two[0:256, :])
    for r in range(2, 8):
        part = low[r * 64 : (r + 1) * 64, :] if r < 4 else high[(r - 4) * 64 : (r - 3) * 64, :]
        field += dot(part, kernel_two[(r - 1) * 256 : r * 256, :])
    total = dot_t(field.astype(BF), lift[...])
    total += dot(sibs_a[64:128, :], kernel_one[0:256, :])
    total += dot(sibs_b[0:64, :], kernel_one[256:512, :])
    total += dot(sibs_b[64:128, :], kernel_one[512:768, :])
    out[...] = total.astype(BF)


def join_body(mine, got, out):
    u = place()[1]
    out[pl.ds(pl.multiple_of(u * 64, 64), 64), :] = mine[...]
    out[pl.ds(pl.multiple_of((1 - u) * 64, 64), 64), :] = got[...]


def add_near(total, left, right, values, base, n):
    for c in range(0, n, 256):
        tile = gauss(left, right[c : c + 256, :])
        part = dot(tile, values[base + c : base + c + 256, :])
        total = part if total is None else total + part
    return total


def own_body(first, own_l, own_r, buf_zero, buf_one, buf_two, buf_three, acc):
    for r in range(0, HALF, 512):
        left = own_l[first + r : first + r + 512, :]
        total = None
        for values, (start, n), base in zip((buf_zero, buf_one, buf_two, buf_three), CHUNKS, BASES):
            total = add_near(total, left, own_r.at[start : start + n, :], values, base, n)
        acc[r : r + 512, :] = total


def chunk_body(i, own_l, pts_a, rhs_a, pts_b, rhs_b, in_a, in_b, acc_a, acc_b, right):
    (start, n), base = CHUNKS[i], BASES[i]
    right[0:n, :] = widened(pts_a[start : start + n, :], False)
    right[n:, :] = widened(pts_b[start : start + n, :], False)
    for r in range(0, LEAF, 512):
        acc_in, acc = (in_a, acc_a) if r < HALF else (in_b, acc_b)
        rows = slice(r % HALF, r % HALF + 512)
        left = own_l[r : r + 512, :]
        total = add_near(acc_in[rows, :], left, right.at[0:n, :], rhs_a, base, n)
        acc[rows, :] = add_near(total, left, right.at[n : 2 * n, :], rhs_b, base, n)


def last_body(
    own_l, pts_a, rhs_a, pts_b, rhs_b, acc_a, acc_b, bases, far, proxy, lift, half, got,
    out, right, node,
):
    start, n = CHUNKS[3]
    core = place()[0]
    z_far = jnp.concatenate([far[RANK:FAR, 0:D], far[RANK:FAR, D:]], axis=0)
    kernel = gauss(widened(z_far, True), widened(proxy[...].astype(BF), False))
    node[pl.ds(pl.multiple_of(core * 128, 128), 128), :] = half[...]
    node[pl.ds(pl.multiple_of((1 - core) * 128, 128), 128), :] = got[...]
    field = dot(far[0:RANK, :], kernel) + dot_t(node[...], lift[...].astype(BF))
    field = field.astype(BF)
    right[0:n, :] = widened(pts_a[start : start + n, :], False)
    right[n:, :] = widened(pts_b[start : start + n, :], False)
    for r in range(0, LEAF, 512):
        left = own_l[r : r + 512, :]
        acc = acc_a if r < HALF else acc_b
        total = acc[r % HALF : r % HALF + 512, :] + dot_t(bases[r : r + 512, :], field)
        total = add_near(total, left, right.at[0:n, :], rhs_a, 0, n)
        total = add_near(total, left, right.at[n : 2 * n, :], rhs_b, 0, n)
        out[r : r + 512, :] = total.astype(BF)


def after(x, token):
    return lax.optimization_barrier((x, token))[0]


def swap(x, flip):
    n = lax.axis_size(AXIS)
    return lax.ppermute(x, AXIS, [(i, i ^ flip) for i in range(n)])


def per_device(
    points, charges, order, near, bases, lift_leaf, lift_node, proxy_leaf, proxy_node, proxy_top
):
    vm, sem = pltpu.VMEM, pltpu.SemaphoreType.DMA

    def choose(got, own, skip=0):
        return call(
            functools.partial(choose_body, skip), [(own.shape, BF)], near, got, own, name="choose", smem=1
        )[0]

    def chunk(i, v):
        n = CHUNKS[i][1]
        return call(
            functools.partial(chunk_body, i), [((HALF, NRHS), F32)] * 2,
            v["own_l"], v["pts_a"], v["far_rows", i], v["pts_b"], v["near_rows", i], v["acc", 0], v["acc", 1],
            name="near_chunk", scratch=[vm((2 * n, 256), BF)], aliases={5: 0, 6: 1},
        )

    def own_half(i, v):
        return call(
            functools.partial(own_body, i * HALF), [((HALF, NRHS), F32)],
            v["own_l"], v["own_r"], *[v["buf", j] for j in range(4)], name="near_own",
        )[0]

    def cat(one, two):
        shape = (2 * one.shape[0], *one.shape[1:])
        return call(cat_body, [(shape, BF)], one, two, name="join_rows")[0]

    v = {}

    def finish(**new):
        v.update(new)
        keys = list(v)
        for key, value in zip(keys, lax.optimization_barrier([v[key] for key in keys])):
            v[key] = value

    stat, = call(
        pack_body, [((208, 128), BF)], lift_node, proxy_node, proxy_top, name="pack", hbm=(0, 1, 2),
        scratch=[vm((64, 256), F32), vm((64, 128), F32), vm((16, 128), F32), sem((3,))],
    )
    finish(stat=stat, order=order, points=points)

    stats = [v["stat"]] + [swap(v["stat"], k) for k in (1, 2, 3)]
    across_a = swap(v["points"][:HALF], 3)
    own_l, own_r, *bufs, keep, send = call(
        prep_body,
        [((LEAF, 256), BF), ((LEAF, 256), BF)]
        + [((base + n, 256), BF) for (_, n), base in zip(CHUNKS, BASES)]
        + [((128, 256), F32), ((128, 256), BF)],
        v["order"], points, charges, bases, lift_leaf, proxy_leaf,
        name="prep", hbm=(1, 2, 3, 4, 5),
        scratch=[
            vm((LEAF, D), BF), vm((LEAF, 256), BF), vm((LEAF, 256), BF), vm((256, 256), F32),
            vm((256, 128), F32), vm((256, 256), F32), sem((5,)),
        ],
    )
    v.update({("buf", i): buf for i, buf in enumerate(bufs)})
    finish(stats=tuple(stats), own_l=own_l, own_r=own_r, keep=keep, send=send)

    got = swap(v["send"], 1)
    z_a, = call(cat_z_body, [((4, 80, 128), BF)], *v["stats"], name="cat_z")
    z_b = swap(z_a, 6)
    finish(got=got, z_a=z_a)

    kept, send = call(
        halve_body, [((64, 256), F32), ((64, 256), BF)], v["keep"], v["got"],
        name="halve", scratch=[vm((128, 256), F32)],
    )
    got = swap(send, 2)
    v["acc", 0] = own_half(0, v)
    across_b = swap(after(v["points"], v["acc", 0])[HALF:], 3)
    finish(got=got, kept=kept, z_b=z_b, across_a=across_a)

    send, lift_all = call(
        node_body, [((128, 256), BF), ((256, 256), BF)], v["kept"], v["got"], *v["stats"], name="node",
    )
    got = swap(send, 6)
    z_c = cat(v["z_a"], v["z_b"])
    z_d = swap(z_c, 8)
    rows = [swap(v["buf", 0], 3)]
    v["acc", 1] = own_half(1, v)
    finish(got=got, send=send, lift_all=lift_all, z_c=z_c, z_d=z_d)

    send, = call(pair_body, [((192, 256), BF)], v["send"], v["got"], name="pair")
    got = swap(send, 8)
    t_a, = call(tops_body, [((16, 16, 128), BF)], v["z_c"], v["z_d"], name="tops")
    t_b = swap(t_a, 24)
    rows.append(swap(v["buf", 1], 3))
    kernel_one, = call(
        node_coupling_body, [((768, 256), BF)], v["z_c"], v["z_d"], name="node_coupling",
        scratch=[vm((1024, 128), BF)],
    )
    pts_a = jnp.concatenate([v["across_a"], across_b], axis=0)
    pts_b = swap(choose(pts_a, v["points"]), 1)
    finish(send_four=send, got_four=got, t_a=t_a, t_b=t_b, kernel_one=kernel_one, pts_a=pts_a)

    top, = call(top_body, [((64, 256), BF)], v["send_four"], v["got_four"], name="top")
    got = swap(top, 24)
    t_a = cat(v["t_a"], v["t_b"])
    t_b = swap(t_a, 32)
    rows.append(swap(v["buf", 2], 3))
    near_rows = [swap(choose(rows[0], v["buf", 0], BASES[0]), 1)]
    v["far_rows", 0] = rows[0]
    finish(got=got, low=top, t_a=t_a, t_b=t_b, pts_b=pts_b)

    low = cat(v["low"], v["got"])
    got = swap(low, 32)
    t_a = cat(v["t_a"], v["t_b"])
    t_b = swap(t_a, 96)
    rows.append(swap(v["buf", 3], 3))
    v["near_rows", 0] = near_rows[0]
    v["acc", 0], v["acc", 1] = chunk(0, v)
    finish(got=got, low=low, t_a=t_a, t_b=t_b)

    low = cat(v["low"], v["got"])
    got = swap(low, 96)
    kernel_two, = call(
        top_coupling_body, [((1792, 256), BF)], v["t_a"], v["t_b"], name="top_coupling",
        scratch=[vm((2048, 128), BF)],
    )
    near_rows.append(swap(choose(rows[1], v["buf", 1], BASES[1]), 1))
    v["far_rows", 1] = rows[1]
    finish(got=got, low=low, kernel_two=kernel_two)

    quarter, = call(
        field_body, [((64, 256), BF)], v["send_four"], v["got_four"], v["low"], v["got"],
        v["kernel_one"], v["kernel_two"], v["lift_all"], name="field",
    )
    got = swap(quarter, 2)
    v["near_rows", 1] = near_rows[1]
    v["acc", 0], v["acc", 1] = chunk(1, v)
    near_rows.append(swap(choose(rows[2], v["buf", 2], BASES[2]), 1))
    v["far_rows", 2] = rows[2]
    finish(got=got, quarter=quarter)

    half, = call(join_body, [((128, 256), BF)], v["quarter"], v["got"], name="join")
    got = swap(half, 1)
    v["near_rows", 2] = near_rows[2]
    v["acc", 0], v["acc", 1] = chunk(2, v)
    near_rows.append(swap(choose(rows[3], v["buf", 3], BASES[3]), 1))
    finish(got=got, half=half)

    n = CHUNKS[3][1]
    out, = call(
        last_body, [((LEAF, NRHS), BF)],
        v["own_l"], v["pts_a"], rows[3], v["pts_b"], near_rows[3], v["acc", 0], v["acc", 1], bases,
        v["near_rows", 1], proxy_leaf, lift_leaf, v["half"], v["got"],
        name="near_last", scratch=[vm((2 * n, 256), BF), vm((256, 256), BF)],
    )
    return out


def solution(mesh):
    spec = P(AXIS, None)
    return jax.shard_map(
        per_device, mesh=mesh, in_specs=(spec,) * 10, out_specs=spec, check_vma=False
    )
```

```python
import functools

import jax
import jax.numpy as jnp
from jax import lax
from jax.experimental import pallas as pl
from jax.experimental.pallas import tpu as pltpu
from jax.sharding import PartitionSpec as P

D = 128
NRHS = 256
RANK = 256
LEAF = 2048
AXIS = "leaf"
BF = jnp.bfloat16
F32 = jnp.float32
SCALE = 4.0 / D * 1.4426950408889634
FAR = 384
CHUNKS = ((0, 768), (768, 768), (1536, 512))
BASES = (0, FAR, 0)
HALF = LEAF // 2


def dot(a, b):
    return lax.dot_general(a, b, (((1,), (0,)), ((), ())), preferred_element_type=F32)


def dot_t(a, b):
    return lax.dot_general(a, b, (((1,), (1,)), ((), ())), preferred_element_type=F32)


def widened(x, left):
    wide = x.astype(F32)
    rest = 0.5 * jnp.sum(wide * wide, axis=1, keepdims=True)
    high = rest.astype(BF).astype(F32)
    rest = rest - high
    middle = rest.astype(BF).astype(F32)
    low = rest - middle
    lane = lax.broadcasted_iota(jnp.int32, (x.shape[0], 128), 1)
    first, ones = (0, 3) if left else (3, 0)
    extra = jnp.where(
        lane == first, -high, jnp.where(lane == first + 1, -middle, jnp.where(lane == first + 2, -low, 0.0))
    )
    extra = jnp.where((lane >= ones) & (lane < ones + 3), 1.0, extra)
    return jnp.concatenate([x.astype(BF), extra.astype(BF)], axis=1)


def gauss(left, right):
    return jnp.exp2(dot_t(left, right) * SCALE).astype(BF)


def call(body, outs, *args, name, scratch=(), smem=0, hbm=(), aliases=None, limit=24):
    def space(i):
        return pltpu.SMEM if i < smem else pltpu.HBM if i in hbm else pltpu.VMEM

    args = [
        pltpu.with_memory_space_constraint(arg, pltpu.HBM) if i in hbm else arg for i, arg in enumerate(args)
    ]
    return pl.pallas_call(
        body,
        out_shape=[jax.ShapeDtypeStruct(s, d) for s, d in outs],
        in_specs=[pl.BlockSpec(memory_space=space(i)) for i in range(len(args))],
        out_specs=[pl.BlockSpec(memory_space=pltpu.VMEM)] * len(outs),
        scratch_shapes=list(scratch),
        input_output_aliases=aliases or {},
        name=name,
        cost_estimate=pl.CostEstimate(flops=0, bytes_accessed=0, transcendentals=0),
        compiler_params=pltpu.CompilerParams(vmem_limit_bytes=limit << 20),
    )(*args)


def place():
    me = lax.axis_index(AXIS)
    x = lax.rem(lax.div(me, 2), 4)
    return lax.rem(me, 2), lax.rem(x, 2) ^ lax.div(x, 2), lax.rem(me, 4), lax.rem(me, 16)


def far_is_core(near):
    slot = place()[2]
    return ((6 - slot - lax.rem(near[0, 0], 4) - lax.rem(near[0, 1], 4)) ^ slot) == 1


def fetched(pairs, sems):
    copies = [pltpu.make_async_copy(src, dst, sems.at[i]) for i, (src, dst) in enumerate(pairs)]
    for copy in copies:
        copy.start()
    return copies


def prep_body(
    order_h, points_h, charges_h, bases_h, lift_h, proxy_h, lift_node_h, proxy_node_h, proxy_top_h,
    own_l, own_r, whole, buf_zero, buf_one, buf_two,
    keep, send, z_out, lift_low, proxy_wide,
    order, points, charges, bases, lift, proxy, lift_node, proxy_node, proxy_top, up, sems,
):
    core = place()[0]
    copies = fetched(
        (
            (order_h, order), (charges_h, charges), (points_h, points), (bases_h, bases), (lift_h, lift), (proxy_h, proxy),
            (lift_node_h, lift_node), (proxy_node_h, proxy_node), (proxy_top_h, proxy_top),
        ),
        sems,
    )
    copies[0].wait()
    rows = [order[:, b * 128 : (b + 1) * 128] for b in range(LEAF // 128)]
    tall = jnp.concatenate(rows * (128 // len(rows)), axis=0).astype(F32).T
    places = lax.broadcasted_iota(jnp.int32, (128, LEAF), 1).astype(F32)
    copies[1].wait()
    for b in range(LEAF // 128):
        hot = jnp.where(tall[:, b : b + 1] == places, 1.0, 0.0).astype(BF)
        whole[FAR + b * 128 : FAR + (b + 1) * 128, :] = dot(hot, charges[...]).astype(BF)
    for copy in copies[2:]:
        copy.wait()
    coef = lax.dot_general(
        whole[FAR:, :], bases[...], (((0,), (0,)), ((), ())), preferred_element_type=F32
    ).astype(BF)
    lift_low[...] = lift[...].astype(BF)
    proxy_wide[...] = widened(proxy[...].astype(BF), False)
    up[...] = dot(coef, lift_low[...])
    keep[...] = up[pl.ds(pl.multiple_of(core * 128, 128), 128), :]
    send[0:128, :] = up[pl.ds(pl.multiple_of((1 - core) * 128, 128), 128), :].astype(BF)
    send[128:192, :] = lift_node[...].astype(BF)
    z_out[0:32, 0:D] = proxy_node[0:32, :].astype(BF)
    z_out[0:32, D:] = proxy_node[32:64, :].astype(BF)
    z_out[32:40, 0:D] = proxy_top[0:8, :].astype(BF)
    z_out[32:40, D:] = proxy_top[8:16, :].astype(BF)
    whole[0:RANK, :] = coef
    whole[RANK:FAR, 0:D] = proxy[0:128, :].astype(BF)
    whole[RANK:FAR, D:] = proxy[128:256, :].astype(BF)
    for buf, (start, n), base in zip((buf_zero, buf_one, buf_two), CHUNKS, BASES):
        if base:
            buf[0:base, :] = whole[0:base, :]
        buf[base:, :] = whole[FAR + start : FAR + start + n, :]
    own_l[...] = widened(points[...], True)
    own_r[...] = widened(points[...], False)


def halve_body(keep, sent, got, z_own, kept, send, total):
    u = place()[1]
    total[...] = keep[...] + got[0:128, :].astype(F32)
    kept[...] = total[pl.ds(pl.multiple_of(u * 64, 64), 64), :]
    send[0:64, :] = total[pl.ds(pl.multiple_of((1 - u) * 64, 64), 64), :].astype(BF)
    send[64:128, :] = sent[128:192, :]
    send[128:192, :] = got[128:192, :]
    send[192:232, :] = z_own[...]


def node_body(kept, sent, got, send, lift):
    slot = place()[2]
    for j, (stat, row) in enumerate(((sent, 64), (sent, 128), (got, 64), (got, 128))):
        lift[pl.ds(pl.multiple_of((slot ^ j) * 64, 64), 64), :] = stat[row : row + 64, :]
    node = (kept[...] + got[0:64, :].astype(F32)).astype(BF)
    send[0:64, :] = node
    send[64:128, :] = dot(node, lift[...]).astype(BF)
    send[128:160, :] = sent[192:224, :]
    send[160:192, :] = got[192:224, :]
    send[192:200, :] = sent[224:232, :]
    send[200:208, :] = got[224:232, :]


def top_body(mine, got_x, got_y, got_xy, out, z_out):
    four = (mine, got_x, got_y, got_xy)
    out[0:64, :] = sum(part[64:128, :].astype(F32) for part in four).astype(BF)
    for h, part in enumerate(four):
        out[64 + 16 * h : 80 + 16 * h, :] = part[192:208, :]
        z_out[64 * h : 64 * h + 64, :] = part[128:192, :]


def more_body(mine, got_y, got_z, got_yz, out):
    for r, part in enumerate((mine, got_y, got_z, got_yz)):
        out[64 * r : 64 * r + 64, :] = part[0:64, :]
        out[256 + 64 * r : 320 + 64 * r, :] = part[64:128, :]


def node_coupling_body(z_own, z_got, out, z_node):
    slot = place()[2]
    for h in range(4):
        for core in range(2):
            for j in range(2):
                block = (z_got if core else z_own)[(2 * h + j) * 32 : (2 * h + j + 1) * 32, :]
                at = (slot ^ core ^ (2 * j) ^ (2 * (h % 2))) * 64
                z_node[pl.ds(pl.multiple_of(h * 256 + at, 64), 32), :] = block[:, 0:D]
                z_node[pl.ds(pl.multiple_of(h * 256 + at + 32, 32), 32), :] = block[:, D:]
    own = widened(z_node[0:256, :], False)
    for h in range(1, 4):
        out[(h - 1) * 256 : h * 256, :] = gauss(widened(z_node[h * 256 : (h + 1) * 256, :], True), own)


def field_body(
    sib_x, sib_y, sib_xy, low, high, low_core, high_core, kernel_one, lift, out, z_top
):
    part = place()[3]
    for r in range(8):
        for core in range(2):
            mine = ((low, high), (low_core, high_core))[core][r // 4]
            for k in range(8):
                offset = core ^ (2 * (k % 2)) ^ (6 * (k // 2 % 2)) ^ (8 * (k // 4)) ^ (8 * (r % 2))
                row = 256 + 64 * (r % 4) + 8 * k
                block = mine[row : row + 8, :].astype(F32)
                at = 256 * r + (part ^ offset) * 16
                z_top[pl.ds(pl.multiple_of(at, 16), 8), :] = block[:, 0:D]
                z_top[pl.ds(pl.multiple_of(at + 8, 8), 8), :] = block[:, D:]
    own = widened(z_top[0:256, :], False)
    field = None
    for r in range(1, 8):
        tile = gauss(widened(z_top[r * 256 : (r + 1) * 256, :], True), own)
        part = dot((low, high)[r // 4][64 * (r % 4) : 64 * (r % 4 + 1), :], tile)
        field = part if field is None else field + part
    total = dot_t(field.astype(BF), lift[...])
    for h, sib in enumerate((sib_x, sib_y, sib_xy)):
        total += dot(sib[0:64, :], kernel_one[256 * h : 256 * (h + 1), :])
    out[...] = total.astype(BF)


def join_body(mine, got, out):
    u = place()[1]
    out[pl.ds(pl.multiple_of(u * 64, 64), 64), :] = mine[...]
    out[pl.ds(pl.multiple_of((1 - u) * 64, 64), 64), :] = got[...]


def add_near(total, left, right, values, base, n):
    for c in range(0, n, 256):
        tile = gauss(left, right[c : c + 256, :])
        part = dot(tile, values[base + c : base + c + 256, :])
        total = part if total is None else total + part
    return total


def own_body(first, own_l, own_r, whole, *acc):
    for r in range(0, HALF, 512):
        total = acc[0][r : r + 512, :] if len(acc) > 1 else None
        left = own_l[first + r : first + r + 512, :]
        acc[-1][r : r + 512, :] = add_near(total, left, own_r, whole, FAR, LEAF)


def choose_body(skip, near, got, own, out):
    core = far_is_core(near)
    width = out.shape[1]

    @pl.when(core)
    def _():
        out[skip:, :] = got[skip:, :]
        if skip:
            out[0:skip, :] = own[0:skip, :]

    @pl.when(jnp.logical_not(core))
    def _():
        out[skip:, :] = own[skip:, 0:width]
        if skip:
            out[0:skip, :] = got[0:skip, :]


def chunk_body(i, own_l, pts_a, rows_a, pts_b, rows_b, in_a, in_b, acc_a, acc_b, right):
    (start, n), base = CHUNKS[i], BASES[i]
    right[0:n, :] = widened(pts_a[start : start + n, :], False)
    right[n : 2 * n, :] = widened(pts_b[start : start + n, :], False)
    for r in range(0, LEAF, 512):
        acc_in, acc = ((in_a, acc_a), (in_b, acc_b))[r // HALF]
        rows = slice(r % HALF, r % HALF + 512)
        left = own_l[r : r + 512, :]
        total = add_near(acc_in[rows, :], left, right.at[0:n, :], rows_a, base, n)
        acc[rows, :] = add_near(total, left, right.at[n : 2 * n, :], rows_b, base, n)


def far_body(rows, proxy, out):
    z_far = jnp.concatenate([rows[RANK:FAR, 0:D], rows[RANK:FAR, D:]], axis=0)
    out[...] = dot(rows[0:RANK, :], gauss(widened(z_far, True), proxy[...]))


def last_body(acc_a, acc_b, bases, far, lift, half, got, out, node):
    core = place()[0]
    node[pl.ds(pl.multiple_of(core * 128, 128), 128), :] = half[...]
    node[pl.ds(pl.multiple_of((1 - core) * 128, 128), 128), :] = got[...]
    field = (far[...] + dot_t(node[...], lift[...])).astype(BF)
    for r in range(0, LEAF, 512):
        acc = (acc_a, acc_b)[r // HALF]
        total = acc[r % HALF : r % HALF + 512, :] + dot_t(bases[r : r + 512, :], field)
        out[r : r + 512, :] = total.astype(BF)


def after(x, token):
    return lax.optimization_barrier((x, token))[0]


def swap(x, flip):
    n = lax.axis_size(AXIS)
    return lax.ppermute(x, AXIS, [(i, i ^ flip) for i in range(n)])


def per_device(
    points, charges, order, near, bases, lift_leaf, lift_node, proxy_leaf, proxy_node, proxy_top
):
    vm, sem = pltpu.VMEM, pltpu.SemaphoreType.DMA

    def chosen(got, own, skip=0):
        return call(
            functools.partial(choose_body, skip), [(got.shape, BF)], near, got, own, name="choose", smem=1
        )[0]

    def chunk(i):
        n = CHUNKS[i][1]
        v["acc", 0], v["acc", 1] = call(
            functools.partial(chunk_body, i), [((HALF, NRHS), F32)] * 2,
            v["own_l"], v["pts_a"], v["rows_a", i], v["pts_b"], v["rows_b", i], v["acc", 0], v["acc", 1],
            name="near_chunk", scratch=[vm((2 * n, 256), BF)], aliases={5: 0, 6: 1},
        )

    def own_half(i):
        v["acc", i], = call(
            functools.partial(own_body, i * HALF), [((HALF, NRHS), F32)],
            v["own_l"], v["own_r"], v["whole"], name="near_own",
        )

    v = {}

    def finish(new):
        v.update(new)
        keys = list(v)
        for key, value in zip(keys, lax.optimization_barrier([v[key] for key in keys])):
            v[key] = value

    pts_a = swap(points, 3)
    own_l, own_r, whole, *bufs, keep, send, z_own, lift_low, proxy_wide = call(
        prep_body,
        [((LEAF, 256), BF), ((LEAF, 256), BF), ((FAR + LEAF, 256), BF)]
        + [((base + n, 256), BF) for (_, n), base in zip(CHUNKS, BASES)]
        + [((128, 256), F32), ((192, 256), BF), ((40, 256), BF), ((256, 256), BF), ((256, 256), BF)],
        order, points, charges, bases, lift_leaf, proxy_leaf, lift_node, proxy_node, proxy_top,
        name="prep", hbm=tuple(range(9)),
        scratch=[
            vm((1, LEAF), jnp.int32), vm((LEAF, D), BF), vm((LEAF, 256), BF), vm((LEAF, 256), BF),
            vm((256, 256), F32), vm((256, 128), F32), vm((64, 256), F32), vm((64, 128), F32), vm((16, 128), F32),
            vm((256, 256), F32), sem((9,)),
        ],
    )
    v.update({("buf", i): buf for i, buf in enumerate(bufs)})
    finish(
        dict(
            own_l=own_l, own_r=own_r, whole=whole, keep=keep, send=send, z_own=z_own,
            lift_low=lift_low, proxy_wide=proxy_wide,
        )
    )

    got = swap(v["send"], 1)
    finish(dict(got=got))

    kept, send = call(
        halve_body, [((64, 256), F32), ((232, 256), BF)], v["keep"], v["send"], v["got"], v["z_own"],
        name="halve", scratch=[vm((128, 256), F32)],
    )
    got = swap(send, 2)
    own_half(0)
    own_half(1)
    finish(dict(got=got, kept=kept, send=send, pts_a=pts_a))

    send, lift_all = call(
        node_body, [((208, 256), BF), ((256, 256), BF)], v["kept"], v["send"], v["got"], name="node",
    )
    got = tuple(swap(send, k) for k in (6, 8, 14))
    rows_zero = swap(v["buf", 0], 3)
    v["pts_b"] = swap(chosen(v["pts_a"], v["own_l"]), 1)
    v["rows_a", 0] = rows_zero
    finish(dict(sibs=got, send=send, lift_all=lift_all))

    top, z_all = call(
        top_body, [((128, 256), BF), ((256, 256), BF)], v["send"], *v["sibs"], name="top"
    )
    got = tuple(swap(top, k) for k in (24, 32, 56))
    rows_one = swap(v["buf", 1], 3)
    v["rows_b", 0] = swap(chosen(v["rows_a", 0], v["buf", 0]), 1)
    chunk(0)
    finish(dict(got=got, low=top, z_all=z_all))

    low, = call(more_body, [((512, 256), BF)], v["low"], *v["got"], name="more")
    got = swap(low, 96)
    z_core = swap(v["z_all"], 1)
    low_core = swap(low, 1)
    rows_two = swap(v["buf", 2], 3)
    kernel_one, = call(
        node_coupling_body, [((768, 256), BF)], v["z_all"], z_core, name="node_coupling",
        scratch=[vm((1024, 128), BF)],
    )
    v["rows_a", 1] = rows_one
    finish(dict(got=got, low=low, low_core=low_core, kernel_one=kernel_one))

    high_core = swap(v["got"], 1)
    v["rows_b", 1] = swap(chosen(v["rows_a", 1], v["buf", 1], BASES[1]), 1)
    finish(dict(high_core=high_core))

    quarter, = call(
        field_body, [((64, 256), BF)], *v["sibs"], v["low"], v["got"], v["low_core"],
        v["high_core"], v["kernel_one"], v["lift_all"], name="field", scratch=[vm((2048, 128), F32)],
    )
    got = swap(quarter, 2)
    far, = call(far_body, [((256, 256), F32)], v["rows_b", 1], v["proxy_wide"], name="far")
    chunk(1)
    v["rows_a", 2] = rows_two
    finish(dict(got=got, quarter=quarter, far=far))

    half, = call(join_body, [((128, 256), BF)], v["quarter"], v["got"], name="join")
    v["rows_b", 2] = swap(chosen(v["rows_a", 2], v["buf", 2]), 1)
    got = swap(half, 1)
    chunk(2)
    out, = call(
        last_body, [((LEAF, NRHS), BF)],
        v["acc", 0], v["acc", 1], bases, v["far"], v["lift_low"], half, got,
        name="descent", scratch=[vm((256, 256), BF)],
    )
    return out


def solution(mesh):
    spec = P(AXIS, None)
    return jax.shard_map(
        per_device, mesh=mesh, in_specs=(spec,) * 10, out_specs=spec, check_vma=False
    )
```

```python
import functools

import jax
import jax.numpy as jnp
from jax import lax
from jax.experimental import pallas as pl
from jax.experimental.pallas import tpu as pltpu
from jax.sharding import PartitionSpec as P

D = 128
NRHS = 256
RANK = 256
LEAF = 2048
AXIS = "leaf"
BF = jnp.bfloat16
F32 = jnp.float32
SCALE = 4.0 / D * 1.4426950408889634
FAR = 384
CHUNKS = ((0, 768), (768, 768), (1536, 512))
BASES = (FAR, 0, 0)
HALF = LEAF // 2


def dot(a, b):
    return lax.dot_general(a, b, (((1,), (0,)), ((), ())), preferred_element_type=F32)


def dot_t(a, b):
    return lax.dot_general(a, b, (((1,), (1,)), ((), ())), preferred_element_type=F32)


def widened(x, left):
    wide = x.astype(F32)
    rest = 0.5 * jnp.sum(wide * wide, axis=1, keepdims=True)
    high = rest.astype(BF).astype(F32)
    rest = rest - high
    middle = rest.astype(BF).astype(F32)
    low = rest - middle
    lane = lax.broadcasted_iota(jnp.int32, (x.shape[0], 128), 1)
    first, ones = (0, 3) if left else (3, 0)
    extra = jnp.where(
        lane == first, -high, jnp.where(lane == first + 1, -middle, jnp.where(lane == first + 2, -low, 0.0))
    )
    extra = jnp.where((lane >= ones) & (lane < ones + 3), 1.0, extra)
    return jnp.concatenate([x.astype(BF), extra.astype(BF)], axis=1)


def gauss(left, right):
    return jnp.exp2(dot_t(left, right) * SCALE).astype(BF)


def call(body, outs, *args, name, scratch=(), smem=0, hbm=(), aliases=None, out_space=pltpu.VMEM):
    def space(i):
        return pltpu.SMEM if i < smem else pltpu.HBM if i in hbm else pltpu.VMEM

    args = [
        pltpu.with_memory_space_constraint(arg, pltpu.HBM) if i in hbm else arg for i, arg in enumerate(args)
    ]
    return pl.pallas_call(
        body,
        out_shape=[jax.ShapeDtypeStruct(s, d) for s, d in outs],
        in_specs=[pl.BlockSpec(memory_space=space(i)) for i in range(len(args))],
        out_specs=[pl.BlockSpec(memory_space=out_space)] * len(outs),
        scratch_shapes=list(scratch),
        input_output_aliases=aliases or {},
        name=name,
        cost_estimate=pl.CostEstimate(flops=0, bytes_accessed=0, transcendentals=0),
        compiler_params=pltpu.CompilerParams(vmem_limit_bytes=24 << 20),
    )(*args)


def place():
    me = lax.axis_index(AXIS)
    x = lax.rem(lax.div(me, 2), 4)
    return lax.rem(me, 2), lax.rem(x, 2) ^ lax.div(x, 2), lax.rem(me, 4), lax.rem(me, 16)


def far_is_core(near):
    slot = place()[2]
    return ((6 - slot - lax.rem(near[0, 0], 4) - lax.rem(near[0, 1], 4)) ^ slot) == 1


def fetched(pairs, sems):
    copies = [pltpu.make_async_copy(src, dst, sems.at[i]) for i, (src, dst) in enumerate(pairs)]
    for copy in copies:
        copy.start()
    return copies


def prep_body(
    order_h, points_h, charges_h, bases_h, lift_h, proxy_h, lift_node_h, proxy_node_h, proxy_top_h,
    own_l, own_r, whole, buf_zero, buf_one, buf_two,
    keep, send, z_out, lift_low, proxy_wide,
    order, points, charges, bases, lift, proxy, lift_node, proxy_node, proxy_top, up, sems,
):
    core = place()[0]
    copies = fetched(
        (
            (order_h, order), (charges_h, charges), (points_h, points), (bases_h, bases), (lift_h, lift), (proxy_h, proxy),
            (lift_node_h, lift_node), (proxy_node_h, proxy_node), (proxy_top_h, proxy_top),
        ),
        sems,
    )
    copies[0].wait()
    rows = [order[:, b * 128 : (b + 1) * 128] for b in range(LEAF // 128)]
    tall = jnp.concatenate(rows * (128 // len(rows)), axis=0).astype(F32).T
    places = lax.broadcasted_iota(jnp.int32, (128, LEAF), 1).astype(F32)
    copies[1].wait()
    for b in range(LEAF // 128):
        hot = jnp.where(tall[:, b : b + 1] == places, 1.0, 0.0).astype(BF)
        whole[FAR + b * 128 : FAR + (b + 1) * 128, :] = dot(hot, charges[...]).astype(BF)
    for copy in copies[2:]:
        copy.wait()
    coef = lax.dot_general(
        whole[FAR:, :], bases[...], (((0,), (0,)), ((), ())), preferred_element_type=F32
    ).astype(BF)
    lift_low[...] = lift[...].astype(BF)
    proxy_wide[...] = widened(proxy[...].astype(BF), False)
    up[...] = dot(coef, lift_low[...])
    keep[...] = up[pl.ds(pl.multiple_of(core * 128, 128), 128), :]
    send[0:128, :] = up[pl.ds(pl.multiple_of((1 - core) * 128, 128), 128), :].astype(BF)
    send[128:192, :] = lift_node[...].astype(BF)
    z_out[0:32, 0:D] = proxy_node[0:32, :].astype(BF)
    z_out[0:32, D:] = proxy_node[32:64, :].astype(BF)
    z_out[32:40, 0:D] = proxy_top[0:8, :].astype(BF)
    z_out[32:40, D:] = proxy_top[8:16, :].astype(BF)
    whole[0:RANK, :] = coef
    whole[RANK:FAR, 0:D] = proxy[0:128, :].astype(BF)
    whole[RANK:FAR, D:] = proxy[128:256, :].astype(BF)
    for buf, (start, n), base in zip((buf_zero, buf_one, buf_two), CHUNKS, BASES):
        if base:
            buf[0:base, :] = whole[0:base, :]
        buf[base:, :] = whole[FAR + start : FAR + start + n, :]
    own_l[...] = widened(points[...], True)
    own_r[...] = widened(points[...], False)


def halve_body(keep, sent, got, z_own, kept, send, total):
    u = place()[1]
    total[...] = keep[...] + got[0:128, :].astype(F32)
    kept[...] = total[pl.ds(pl.multiple_of(u * 64, 64), 64), :]
    send[0:64, :] = total[pl.ds(pl.multiple_of((1 - u) * 64, 64), 64), :].astype(BF)
    send[64:128, :] = sent[128:192, :]
    send[128:192, :] = got[128:192, :]
    send[192:232, :] = z_own[...]


def node_body(kept, sent, got, send, lift):
    slot = place()[2]
    for j, (stat, row) in enumerate(((sent, 64), (sent, 128), (got, 64), (got, 128))):
        lift[pl.ds(pl.multiple_of((slot ^ j) * 64, 64), 64), :] = stat[row : row + 64, :]
    node = (kept[...] + got[0:64, :].astype(F32)).astype(BF)
    send[0:64, :] = node
    send[64:128, :] = dot(node, lift[...]).astype(BF)
    send[128:160, :] = sent[192:224, :]
    send[160:192, :] = got[192:224, :]
    send[192:200, :] = sent[224:232, :]
    send[200:208, :] = got[224:232, :]


def top_body(mine, got_x, got_y, got_xy, out, z_out, t_out):
    four = (mine, got_x, got_y, got_xy)
    out[0:64, :] = sum(part[64:128, :].astype(F32) for part in four).astype(BF)
    for h, part in enumerate(four):
        out[64 + 16 * h : 80 + 16 * h, :] = part[192:208, :]
        t_out[16 * h : 16 * h + 16, :] = part[192:208, :]
        z_out[64 * h : 64 * h + 64, :] = part[128:192, :]


def more_body(mine, got_y, got_z, got_yz, z_all, out, side):
    for r, part in enumerate((mine, got_y, got_z, got_yz)):
        out[64 * r : 64 * r + 64, :] = part[0:64, :]
        side[64 * r : 64 * r + 64, :] = part[64:128, :]
    side[256:, :] = z_all[...]


def node_coupling_body(z_own, z_got, out, z_node):
    slot = place()[2]
    for h in range(4):
        for core in range(2):
            for j in range(2):
                row = (256 if core else 0) + (2 * h + j) * 32
                block = (z_got if core else z_own)[row : row + 32, :]
                at = (slot ^ core ^ (2 * j) ^ (2 * (h % 2))) * 64
                z_node[pl.ds(pl.multiple_of(h * 256 + at, 64), 32), :] = block[:, 0:D]
                z_node[pl.ds(pl.multiple_of(h * 256 + at + 32, 32), 32), :] = block[:, D:]
    own = widened(z_node[0:256, :], False)
    for h in range(1, 4):
        out[(h - 1) * 256 : h * 256, :] = gauss(widened(z_node[h * 256 : (h + 1) * 256, :], True), own)


def top_coupling_body(low, side, side_core, across, across_core, own_field, send, z_top):
    part = place()[3]
    for r in range(5):
        for core in range(2):
            for k in range(8):
                offset = core ^ (2 * (k % 2)) ^ (6 * (k // 2 % 2)) ^ (8 * (k // 4)) ^ (8 * (r % 2))
                rows, first = ((across, across_core), 0) if r == 4 else ((side, side_core), 64 * r)
                block = rows[core][first + 8 * k : first + 8 * k + 8, :].astype(F32)
                at = 256 * r + (part ^ offset) * 16
                z_top[pl.ds(pl.multiple_of(at, 16), 8), :] = block[:, 0:D]
                z_top[pl.ds(pl.multiple_of(at + 8, 8), 8), :] = block[:, D:]
    own = widened(z_top[0:256, :], False)
    other = widened(z_top[1024:1280, :], False)
    sums = [None, None]
    for r in range(4):
        left = widened(z_top[r * 256 : (r + 1) * 256, :], True)
        for i, right in enumerate((own, other)):
            if r or i:
                term = dot(low[64 * r : 64 * r + 64, :], gauss(left, right))
                sums[i] = term if sums[i] is None else sums[i] + term
    own_field[...] = sums[0]
    send[...] = sums[1].astype(BF)


def field_body(sib_x, sib_y, sib_xy, own_field, got, kernel_one, lift, out):
    total = dot_t((own_field[...] + got[...].astype(F32)).astype(BF), lift[...])
    for h, sib in enumerate((sib_x, sib_y, sib_xy)):
        total += dot(sib[0:64, :], kernel_one[256 * h : 256 * (h + 1), :])
    out[...] = total.astype(BF)


def join_body(mine, got, out):
    u = place()[1]
    out[pl.ds(pl.multiple_of(u * 64, 64), 64), :] = mine[...]
    out[pl.ds(pl.multiple_of((1 - u) * 64, 64), 64), :] = got[...]


def add_near(total, left, right, values, base, n):
    for c in range(0, n, 256):
        tile = gauss(left, right[c : c + 256, :])
        part = dot(tile, values[base + c : base + c + 256, :])
        total = part if total is None else total + part
    return total


def own_body(first, own_l, own_r, whole, *acc):
    for r in range(0, HALF, 512):
        total = acc[0][r : r + 512, :] if len(acc) > 1 else None
        left = own_l[first + r : first + r + 512, :]
        acc[-1][r : r + 512, :] = add_near(total, left, own_r, whole, FAR, LEAF)


def choose_body(skip, near, got, own, out):
    core = far_is_core(near)
    width = out.shape[1]

    @pl.when(core)
    def _():
        out[skip:, :] = got[skip:, :]
        if skip:
            out[0:skip, :] = own[0:skip, :]

    @pl.when(jnp.logical_not(core))
    def _():
        out[skip:, :] = own[skip:, 0:width]
        if skip:
            out[0:skip, :] = got[0:skip, :]


def chunk_body(i, own_l, pts_a, rows_a, pts_b, rows_b, in_a, in_b, acc_a, acc_b, right):
    (start, n), base = CHUNKS[i], BASES[i]
    right[0:n, :] = widened(pts_a[start : start + n, :], False)
    right[n : 2 * n, :] = widened(pts_b[start : start + n, :], False)
    for r in range(0, LEAF, 512):
        acc_in, acc = ((in_a, acc_a), (in_b, acc_b))[r // HALF]
        rows = slice(r % HALF, r % HALF + 512)
        left = own_l[r : r + 512, :]
        total = add_near(acc_in[rows, :], left, right.at[0:n, :], rows_a, base, n)
        acc[rows, :] = add_near(total, left, right.at[n : 2 * n, :], rows_b, base, n)


def far_body(rows, proxy, out):
    z_far = jnp.concatenate([rows[RANK:FAR, 0:D], rows[RANK:FAR, D:]], axis=0)
    out[...] = dot(rows[0:RANK, :], gauss(widened(z_far, True), proxy[...]))


def last_body(in_a, in_b, bases, far, lift, half, got, out_h, node, out, sems):
    core = place()[0]
    node[pl.ds(pl.multiple_of(core * 128, 128), 128), :] = half[...]
    node[pl.ds(pl.multiple_of((1 - core) * 128, 128), 128), :] = got[...]
    field = (far[...] + dot_t(node[...], lift[...])).astype(BF)
    copies = []
    for r in range(0, LEAF, 256):
        total = (in_a, in_b)[r // HALF][r % HALF : r % HALF + 256, :] + dot_t(bases[r : r + 256, :], field)
        out[r : r + 256, :] = total.astype(BF)
        copies.append(
            pltpu.make_async_copy(out.at[r : r + 256, :], out_h.at[r : r + 256, :], sems.at[r // 256])
        )
        copies[-1].start()
    for copy in copies:
        copy.wait()


def after(x, token):
    return lax.optimization_barrier((x, token))[0]


def swap(x, flip):
    n = lax.axis_size(AXIS)
    return lax.ppermute(x, AXIS, [(i, i ^ flip) for i in range(n)])


def per_device(
    points, charges, order, near, bases, lift_leaf, lift_node, proxy_leaf, proxy_node, proxy_top
):
    vm, sem = pltpu.VMEM, pltpu.SemaphoreType.DMA

    def chosen(got, own, skip=0):
        return call(
            functools.partial(choose_body, skip), [(got.shape, BF)], near, got, own, name="choose", smem=1
        )[0]

    def chunk(i):
        n = CHUNKS[i][1]
        v["acc", 0], v["acc", 1] = call(
            functools.partial(chunk_body, i), [((HALF, NRHS), F32)] * 2,
            v["own_l"], v["pts_a"], v["rows_a", i], v["pts_b"], v["rows_b", i], v["acc", 0], v["acc", 1],
            name="near_chunk", scratch=[vm((2 * n, 256), BF)], aliases={5: 0, 6: 1},
        )

    def own_half(i):
        v["acc", i], = call(
            functools.partial(own_body, i * HALF), [((HALF, NRHS), F32)],
            v["own_l"], v["own_r"], v["whole"], name="near_own",
        )

    v = {}

    def finish(new):
        v.update(new)
        keys = list(v)
        for key, value in zip(keys, lax.optimization_barrier([v[key] for key in keys])):
            v[key] = value

    pts_a = swap(points, 3)
    own_l, own_r, whole, *bufs, keep, send, z_own, lift_low, proxy_wide = call(
        prep_body,
        [((LEAF, 256), BF), ((LEAF, 256), BF), ((FAR + LEAF, 256), BF)]
        + [((base + n, 256), BF) for (_, n), base in zip(CHUNKS, BASES)]
        + [((128, 256), F32), ((192, 256), BF), ((40, 256), BF), ((256, 256), BF), ((256, 256), BF)],
        order, points, charges, bases, lift_leaf, proxy_leaf, lift_node, proxy_node, proxy_top,
        name="prep", hbm=tuple(range(9)),
        scratch=[
            vm((1, LEAF), jnp.int32), vm((LEAF, D), BF), vm((LEAF, 256), BF), vm((LEAF, 256), BF),
            vm((256, 256), F32), vm((256, 128), F32), vm((64, 256), F32), vm((64, 128), F32), vm((16, 128), F32),
            vm((256, 256), F32), sem((9,)),
        ],
    )
    v.update({("buf", i): buf for i, buf in enumerate(bufs)})
    finish(
        dict(
            own_l=own_l, own_r=own_r, whole=whole, keep=keep, send=send, z_own=z_own,
            lift_low=lift_low, proxy_wide=proxy_wide,
        )
    )

    got = swap(v["send"], 1)
    finish(dict(got=got))

    kept, send = call(
        halve_body, [((64, 256), F32), ((232, 256), BF)], v["keep"], v["send"], v["got"], v["z_own"],
        name="halve", scratch=[vm((128, 256), F32)],
    )
    got = swap(send, 2)
    rows_zero = swap(v["buf", 0], 3)
    own_half(0)
    own_half(1)
    finish(dict(got=got, kept=kept, send=send, pts_a=pts_a))

    send, lift_all = call(
        node_body, [((208, 256), BF), ((256, 256), BF)], v["kept"], v["send"], v["got"], name="node",
    )
    got = tuple(swap(send, k) for k in (6, 8, 14))
    v["pts_b"] = swap(chosen(v["pts_a"], v["own_l"]), 1)
    v["rows_a", 0] = rows_zero
    finish(dict(sibs=got, send=send, lift_all=lift_all))

    top, z_all, t_own = call(
        top_body, [((128, 256), BF), ((256, 256), BF), ((64, 256), BF)], v["send"], *v["sibs"], name="top"
    )
    got = tuple(swap(top, k) for k in (24, 32, 56))
    rows_one = swap(v["buf", 1], 3)
    v["rows_b", 0] = swap(chosen(v["rows_a", 0], v["buf", 0], FAR), 1)
    chunk(0)
    finish(dict(got=got, low=top, z_all=z_all, t_own=t_own))

    across = swap(v["t_own"], 96)
    low, side = call(
        more_body, [((256, 256), BF), ((512, 256), BF)], v["low"], *v["got"], v["z_all"], name="more"
    )
    side_core = swap(side, 1)
    rows_two = swap(v["buf", 2], 3)
    far, = call(far_body, [((256, 256), F32)], v["rows_b", 0], v["proxy_wide"], name="far")
    v["rows_a", 1] = rows_one
    finish(dict(low=low, side=side, side_core=side_core, far=far, across=across))

    across_core = swap(v["across"], 1)
    rows_b_one = swap(chosen(v["rows_a", 1], v["buf", 1]), 1)
    kernel_one, = call(
        node_coupling_body, [((768, 256), BF)], v["z_all"], v["side_core"], name="node_coupling",
        scratch=[vm((1024, 128), BF)],
    )
    finish(dict(across_core=across_core, kernel_one=kernel_one))

    own_field, send = call(
        top_coupling_body, [((64, 256), F32), ((64, 256), BF)], v["low"], v["side"], v["side_core"],
        v["across"], v["across_core"], name="top_coupling", scratch=[vm((1280, 128), F32)],
    )
    got = swap(send, 96)
    v["rows_b", 1] = rows_b_one
    chunk(1)
    v["rows_a", 2] = rows_two
    finish(dict(got=got, own_field=own_field))

    quarter, = call(
        field_body, [((64, 256), BF)], *v["sibs"], v["own_field"], v["got"], v["kernel_one"], v["lift_all"],
        name="field",
    )
    got = swap(quarter, 2)
    v["rows_b", 2] = swap(chosen(v["rows_a", 2], v["buf", 2]), 1)
    chunk(2)
    finish(dict(got=got, quarter=quarter))

    half, = call(join_body, [((128, 256), BF)], v["quarter"], v["got"], name="join")
    out, = call(
        last_body, [((LEAF, NRHS), BF)],
        v["acc", 0], v["acc", 1], bases, v["far"], v["lift_low"], half, swap(half, 1),
        name="descent", out_space=pl.ANY, scratch=[vm((256, 256), BF), vm((LEAF, NRHS), BF), sem((8,))],
    )
    return out


def solution(mesh):
    spec = P(AXIS, None)
    return jax.shard_map(
        per_device, mesh=mesh, in_specs=(spec,) * 10, out_specs=spec, check_vma=False
    )
```

```python
import functools

import jax
import jax.numpy as jnp
from jax import lax
from jax.experimental import pallas as pl
from jax.experimental.pallas import tpu as pltpu
from jax.sharding import PartitionSpec as P

D = 128
NRHS = 256
RANK = 256
LEAF = 2048
AXIS = "leaf"
BF = jnp.bfloat16
F32 = jnp.float32
SCALE = 4.0 / D * 1.4426950408889634
FAR = 384
CHUNKS = ((0, 768), (768, 768), (1536, 512))
BASES = (FAR, 0, 0)
HALF = LEAF // 2


def dot(a, b):
    return lax.dot_general(a, b, (((1,), (0,)), ((), ())), preferred_element_type=F32)


def dot_t(a, b):
    return lax.dot_general(a, b, (((1,), (1,)), ((), ())), preferred_element_type=F32)


def widened(x, left):
    wide = x.astype(F32)
    rest = 0.5 * jnp.sum(wide * wide, axis=1, keepdims=True)
    high = rest.astype(BF).astype(F32)
    rest = rest - high
    middle = rest.astype(BF).astype(F32)
    low = rest - middle
    lane = lax.broadcasted_iota(jnp.int32, (x.shape[0], 128), 1)
    first, ones = (0, 3) if left else (3, 0)
    extra = jnp.where(
        lane == first, -high, jnp.where(lane == first + 1, -middle, jnp.where(lane == first + 2, -low, 0.0))
    )
    extra = jnp.where((lane >= ones) & (lane < ones + 3), 1.0, extra)
    return jnp.concatenate([x.astype(BF), extra.astype(BF)], axis=1)


def gauss(left, right):
    return jnp.exp2(dot_t(left, right) * SCALE).astype(BF)


def call(body, outs, *args, name, scratch=(), smem=0, hbm=(), aliases=None, out_space=pltpu.VMEM):
    def space(i):
        return pltpu.SMEM if i < smem else pltpu.HBM if i in hbm else pltpu.VMEM

    args = [
        pltpu.with_memory_space_constraint(arg, pltpu.HBM) if i in hbm else arg for i, arg in enumerate(args)
    ]
    return pl.pallas_call(
        body,
        out_shape=[jax.ShapeDtypeStruct(s, d) for s, d in outs],
        in_specs=[pl.BlockSpec(memory_space=space(i)) for i in range(len(args))],
        out_specs=[pl.BlockSpec(memory_space=out_space)] * len(outs),
        scratch_shapes=list(scratch),
        input_output_aliases=aliases or {},
        name=name,
        cost_estimate=pl.CostEstimate(flops=0, bytes_accessed=0, transcendentals=0),
        compiler_params=pltpu.CompilerParams(vmem_limit_bytes=24 << 20),
    )(*args)


def place():
    me = lax.axis_index(AXIS)
    x = lax.rem(lax.div(me, 2), 4)
    return lax.rem(me, 2), lax.rem(x, 2) ^ lax.div(x, 2), lax.rem(me, 4), lax.rem(me, 16)


def far_is_core(near):
    slot = place()[2]
    return ((6 - slot - lax.rem(near[0, 0], 4) - lax.rem(near[0, 1], 4)) ^ slot) == 1


def fetched(pairs, sems):
    copies = [pltpu.make_async_copy(src, dst, sems.at[i]) for i, (src, dst) in enumerate(pairs)]
    for copy in copies:
        copy.start()
    return copies


def prep_body(
    order_h, points_h, charges_h, bases_h, lift_h, proxy_h, lift_node_h, proxy_node_h, proxy_top_h,
    own_l, own_r, whole, buf_zero, buf_one, buf_two,
    keep, send, z_out, lift_low, proxy_wide,
    order, points, charges, bases, lift, proxy, lift_node, proxy_node, proxy_top, up, sems,
):
    core = place()[0]
    copies = fetched(
        (
            (order_h, order), (charges_h, charges), (points_h, points), (bases_h, bases), (lift_h, lift), (proxy_h, proxy),
            (lift_node_h, lift_node), (proxy_node_h, proxy_node), (proxy_top_h, proxy_top),
        ),
        sems,
    )
    copies[0].wait()
    rows = [order[:, b * 128 : (b + 1) * 128] for b in range(LEAF // 128)]
    tall = jnp.concatenate(rows * (128 // len(rows)), axis=0).astype(F32).T
    places = lax.broadcasted_iota(jnp.int32, (128, LEAF), 1).astype(F32)
    copies[1].wait()
    for b in range(LEAF // 128):
        hot = jnp.where(tall[:, b : b + 1] == places, 1.0, 0.0).astype(BF)
        whole[FAR + b * 128 : FAR + (b + 1) * 128, :] = dot(hot, charges[...]).astype(BF)
    for copy in copies[2:]:
        copy.wait()
    coef = lax.dot_general(
        whole[FAR:, :], bases[...], (((0,), (0,)), ((), ())), preferred_element_type=F32
    ).astype(BF)
    lift_low[...] = lift[...].astype(BF)
    proxy_wide[...] = widened(proxy[...].astype(BF), False)
    up[...] = dot(coef, lift_low[...])
    keep[...] = up[pl.ds(pl.multiple_of(core * 128, 128), 128), :]
    send[0:128, :] = up[pl.ds(pl.multiple_of((1 - core) * 128, 128), 128), :].astype(BF)
    send[128:192, :] = lift_node[...].astype(BF)
    z_out[0:32, 0:D] = proxy_node[0:32, :].astype(BF)
    z_out[0:32, D:] = proxy_node[32:64, :].astype(BF)
    z_out[32:40, 0:D] = proxy_top[0:8, :].astype(BF)
    z_out[32:40, D:] = proxy_top[8:16, :].astype(BF)
    whole[0:RANK, :] = coef
    whole[RANK:FAR, 0:D] = proxy[0:128, :].astype(BF)
    whole[RANK:FAR, D:] = proxy[128:256, :].astype(BF)
    for buf, (start, n), base in zip((buf_zero, buf_one, buf_two), CHUNKS, BASES):
        if base:
            buf[0:base, :] = whole[0:base, :]
        buf[base:, :] = whole[FAR + start : FAR + start + n, :]
    own_l[...] = widened(points[...], True)
    own_r[...] = widened(points[...], False)


def halve_body(keep, sent, got, z_own, kept, send, total):
    u = place()[1]
    total[...] = keep[...] + got[0:128, :].astype(F32)
    kept[...] = total[pl.ds(pl.multiple_of(u * 64, 64), 64), :]
    send[0:64, :] = total[pl.ds(pl.multiple_of((1 - u) * 64, 64), 64), :].astype(BF)
    send[64:128, :] = sent[128:192, :]
    send[128:192, :] = got[128:192, :]
    send[192:232, :] = z_own[...]


def node_body(kept, sent, got, send, lift):
    slot = place()[2]
    for j, (stat, row) in enumerate(((sent, 64), (sent, 128), (got, 64), (got, 128))):
        lift[pl.ds(pl.multiple_of((slot ^ j) * 64, 64), 64), :] = stat[row : row + 64, :]
    node = (kept[...] + got[0:64, :].astype(F32)).astype(BF)
    send[0:64, :] = node
    send[64:128, :] = dot(node, lift[...]).astype(BF)
    send[128:160, :] = sent[192:224, :]
    send[160:192, :] = got[192:224, :]
    send[192:200, :] = sent[224:232, :]
    send[200:208, :] = got[224:232, :]


def top_body(mine, got_x, got_y, got_xy, out, z_out, t_out):
    four = (mine, got_x, got_y, got_xy)
    out[0:64, :] = sum(part[64:128, :].astype(F32) for part in four).astype(BF)
    for h, part in enumerate(four):
        out[64 + 16 * h : 80 + 16 * h, :] = part[192:208, :]
        t_out[16 * h : 16 * h + 16, :] = part[192:208, :]
        z_out[64 * h : 64 * h + 64, :] = part[128:192, :]


def more_body(mine, got_y, got_z, got_yz, z_all, out, side):
    for r, part in enumerate((mine, got_y, got_z, got_yz)):
        out[64 * r : 64 * r + 64, :] = part[0:64, :]
        side[64 * r : 64 * r + 64, :] = part[64:128, :]
    side[256:, :] = z_all[...]


def node_coupling_body(z_own, z_got, out, z_node):
    slot = place()[2]
    for h in range(4):
        for core in range(2):
            for j in range(2):
                row = (256 if core else 0) + (2 * h + j) * 32
                block = (z_got if core else z_own)[row : row + 32, :]
                at = (slot ^ core ^ (2 * j) ^ (2 * (h % 2))) * 64
                z_node[pl.ds(pl.multiple_of(h * 256 + at, 64), 32), :] = block[:, 0:D]
                z_node[pl.ds(pl.multiple_of(h * 256 + at + 32, 32), 32), :] = block[:, D:]
    own = widened(z_node[0:256, :], False)
    for h in range(1, 4):
        out[(h - 1) * 256 : h * 256, :] = gauss(widened(z_node[h * 256 : (h + 1) * 256, :], True), own)


def top_coupling_body(low, side, side_core, across, across_core, own_field, send, z_top):
    part = place()[3]
    for r in range(5):
        for core in range(2):
            for k in range(8):
                offset = core ^ (2 * (k % 2)) ^ (6 * (k // 2 % 2)) ^ (8 * (k // 4)) ^ (8 * (r % 2))
                rows, first = ((across, across_core), 0) if r == 4 else ((side, side_core), 64 * r)
                block = rows[core][first + 8 * k : first + 8 * k + 8, :].astype(F32)
                at = 256 * r + (part ^ offset) * 16
                z_top[pl.ds(pl.multiple_of(at, 16), 8), :] = block[:, 0:D]
                z_top[pl.ds(pl.multiple_of(at + 8, 8), 8), :] = block[:, D:]
    own = widened(z_top[0:256, :], False)
    other = widened(z_top[1024:1280, :], False)
    sums = [None, None]
    for r in range(4):
        left = widened(z_top[r * 256 : (r + 1) * 256, :], True)
        for i, right in enumerate((own, other)):
            if r or i:
                term = dot(low[64 * r : 64 * r + 64, :], gauss(left, right))
                sums[i] = term if sums[i] is None else sums[i] + term
    own_field[...] = sums[0]
    send[...] = sums[1].astype(BF)


def field_body(sib_x, sib_y, sib_xy, own_field, got, kernel_one, lift, out):
    total = dot_t((own_field[...] + got[...].astype(F32)).astype(BF), lift[...])
    for h, sib in enumerate((sib_x, sib_y, sib_xy)):
        total += dot(sib[0:64, :], kernel_one[256 * h : 256 * (h + 1), :])
    out[...] = total.astype(BF)


def join_body(mine, got, out):
    u = place()[1]
    out[pl.ds(pl.multiple_of(u * 64, 64), 64), :] = mine[...]
    out[pl.ds(pl.multiple_of((1 - u) * 64, 64), 64), :] = got[...]


def add_near(total, left, right, values, base, n):
    for c in range(0, n, 256):
        tile = gauss(left, right[c : c + 256, :])
        part = dot(tile, values[base + c : base + c + 256, :])
        total = part if total is None else total + part
    return total


def own_body(first, own_l, own_r, whole, *acc):
    for r in range(0, HALF, 512):
        total = acc[0][r : r + 512, :] if len(acc) > 1 else None
        left = own_l[first + r : first + r + 512, :]
        acc[-1][r : r + 512, :] = add_near(total, left, own_r, whole, FAR, LEAF)


def choose_body(skip, near, got, own, out):
    core = far_is_core(near)
    width = out.shape[1]

    @pl.when(core)
    def _():
        out[skip:, :] = got[skip:, :]
        if skip:
            out[0:skip, :] = own[0:skip, :]

    @pl.when(jnp.logical_not(core))
    def _():
        out[skip:, :] = own[skip:, 0:width]
        if skip:
            out[0:skip, :] = got[0:skip, :]


def chunk_body(i, own_l, pts_a, rows_a, pts_b, rows_b, in_a, in_b, acc_a, acc_b, right):
    (start, n), base = CHUNKS[i], BASES[i]
    right[0:n, :] = widened(pts_a[start : start + n, :], False)
    right[n : 2 * n, :] = widened(pts_b[start : start + n, :], False)
    for r in range(0, LEAF, 512):
        acc_in, acc = ((in_a, acc_a), (in_b, acc_b))[r // HALF]
        rows = slice(r % HALF, r % HALF + 512)
        left = own_l[r : r + 512, :]
        total = add_near(acc_in[rows, :], left, right.at[0:n, :], rows_a, base, n)
        acc[rows, :] = add_near(total, left, right.at[n : 2 * n, :], rows_b, base, n)


def far_body(rows, proxy, out):
    z_far = jnp.concatenate([rows[RANK:FAR, 0:D], rows[RANK:FAR, D:]], axis=0)
    out[...] = dot(rows[0:RANK, :], gauss(widened(z_far, True), proxy[...]))


def last_body(in_a, in_b, bases, far, lift, half, got, out_h, node, out, sems):
    core = place()[0]
    node[pl.ds(pl.multiple_of(core * 128, 128), 128), :] = half[...]
    node[pl.ds(pl.multiple_of((1 - core) * 128, 128), 128), :] = got[...]
    field = (far[...] + dot_t(node[...], lift[...])).astype(BF)
    copies = []
    for r in range(0, LEAF, 256):
        total = (in_a, in_b)[r // HALF][r % HALF : r % HALF + 256, :] + dot_t(bases[r : r + 256, :], field)
        out[r : r + 256, :] = total.astype(BF)
        copies.append(
            pltpu.make_async_copy(out.at[r : r + 256, :], out_h.at[r : r + 256, :], sems.at[r // 256])
        )
        copies[-1].start()
    for copy in copies:
        copy.wait()


def after(x, token):
    return lax.optimization_barrier((x, token))[0]


def swap(x, flip):
    n = lax.axis_size(AXIS)
    return lax.ppermute(x, AXIS, [(i, i ^ flip) for i in range(n)])


def per_device(
    points, charges, order, near, bases, lift_leaf, lift_node, proxy_leaf, proxy_node, proxy_top
):
    vm, sem = pltpu.VMEM, pltpu.SemaphoreType.DMA

    def chosen(got, own, skip=0):
        return call(
            functools.partial(choose_body, skip), [(got.shape, BF)], near, got, own, name="choose", smem=1
        )[0]

    def chunk(i):
        n = CHUNKS[i][1]
        v["acc", 0], v["acc", 1] = call(
            functools.partial(chunk_body, i), [((HALF, NRHS), F32)] * 2,
            v["own_l"], v["pts_a"], v["rows_a", i], v["pts_b"], v["rows_b", i], v["acc", 0], v["acc", 1],
            name="near_chunk", scratch=[vm((2 * n, 256), BF)], aliases={5: 0, 6: 1},
        )

    def own_half(i):
        v["acc", i], = call(
            functools.partial(own_body, i * HALF), [((HALF, NRHS), F32)],
            v["own_l"], v["own_r"], v["whole"], name="near_own",
        )

    v = {}

    def finish(new):
        v.update(new)
        keys = list(v)
        for key, value in zip(keys, lax.optimization_barrier([v[key] for key in keys])):
            v[key] = value

    pts_a = swap(points, 3)
    own_l, own_r, whole, *bufs, keep, send, z_own, lift_low, proxy_wide = call(
        prep_body,
        [((LEAF, 256), BF), ((LEAF, 256), BF), ((FAR + LEAF, 256), BF)]
        + [((base + n, 256), BF) for (_, n), base in zip(CHUNKS, BASES)]
        + [((128, 256), F32), ((192, 256), BF), ((40, 256), BF), ((256, 256), BF), ((256, 256), BF)],
        order, points, charges, bases, lift_leaf, proxy_leaf, lift_node, proxy_node, proxy_top,
        name="prep", hbm=tuple(range(9)),
        scratch=[
            vm((1, LEAF), jnp.int32), vm((LEAF, D), BF), vm((LEAF, 256), BF), vm((LEAF, 256), BF),
            vm((256, 256), F32), vm((256, 128), F32), vm((64, 256), F32), vm((64, 128), F32), vm((16, 128), F32),
            vm((256, 256), F32), sem((9,)),
        ],
    )
    v.update({("buf", i): buf for i, buf in enumerate(bufs)})
    finish(
        dict(
            own_l=own_l, own_r=own_r, whole=whole, keep=keep, send=send, z_own=z_own,
            lift_low=lift_low, proxy_wide=proxy_wide,
        )
    )

    got = swap(v["send"], 1)
    finish(dict(got=got))

    kept, send = call(
        halve_body, [((64, 256), F32), ((232, 256), BF)], v["keep"], v["send"], v["got"], v["z_own"],
        name="halve", scratch=[vm((128, 256), F32)],
    )
    got = swap(send, 2)
    rows_zero = swap(v["buf", 0], 3)
    own_half(0)
    own_half(1)
    finish(dict(got=got, kept=kept, send=send, pts_a=pts_a))

    send, lift_all = call(
        node_body, [((208, 256), BF), ((256, 256), BF)], v["kept"], v["send"], v["got"], name="node",
    )
    got = tuple(swap(send, k) for k in (6, 8, 14))
    v["pts_b"] = swap(chosen(v["pts_a"], v["own_l"]), 1)
    v["rows_a", 0] = rows_zero
    finish(dict(sibs=got, send=send, lift_all=lift_all))

    top, z_all, t_own = call(
        top_body, [((128, 256), BF), ((256, 256), BF), ((64, 256), BF)], v["send"], *v["sibs"], name="top"
    )
    got = tuple(swap(top, k) for k in (24, 32, 56))
    rows_one = swap(v["buf", 1], 3)
    v["rows_b", 0] = swap(chosen(v["rows_a", 0], v["buf", 0], FAR), 1)
    chunk(0)
    finish(dict(got=got, low=top, z_all=z_all, t_own=t_own))

    across, across_core = swap(v["t_own"], 96), swap(v["t_own"], 97)
    low, side = call(
        more_body, [((256, 256), BF), ((512, 256), BF)], v["low"], *v["got"], v["z_all"], name="more"
    )
    side_core = swap(side, 1)
    rows_two = swap(v["buf", 2], 3)
    far, = call(far_body, [((256, 256), F32)], v["rows_b", 0], v["proxy_wide"], name="far")
    v["rows_a", 1] = rows_one
    finish(dict(low=low, side=side, side_core=side_core, far=far, across=across, across_core=across_core))

    own_field, send = call(
        top_coupling_body, [((64, 256), F32), ((64, 256), BF)], v["low"], v["side"], v["side_core"],
        v["across"], v["across_core"], name="top_coupling", scratch=[vm((1280, 128), F32)],
    )
    got = swap(send, 96)
    v["rows_b", 1] = swap(chosen(v["rows_a", 1], v["buf", 1]), 1)
    kernel_one, = call(
        node_coupling_body, [((768, 256), BF)], v["z_all"], v["side_core"], name="node_coupling",
        scratch=[vm((1024, 128), BF)],
    )
    chunk(1)
    v["rows_a", 2] = rows_two
    finish(dict(got=got, own_field=own_field, kernel_one=kernel_one))

    quarter, = call(
        field_body, [((64, 256), BF)], *v["sibs"], v["own_field"], v["got"], v["kernel_one"], v["lift_all"],
        name="field",
    )
    got = swap(quarter, 2)
    v["rows_b", 2] = swap(chosen(v["rows_a", 2], v["buf", 2]), 1)
    chunk(2)
    finish(dict(got=got, quarter=quarter))

    half, = call(join_body, [((128, 256), BF)], v["quarter"], v["got"], name="join")
    out, = call(
        last_body, [((LEAF, NRHS), BF)],
        v["acc", 0], v["acc", 1], bases, v["far"], v["lift_low"], half, swap(half, 1),
        name="descent", out_space=pl.ANY, scratch=[vm((256, 256), BF), vm((LEAF, NRHS), BF), sem((8,))],
    )
    return out


def solution(mesh):
    spec = P(AXIS, None)
    return jax.shard_map(
        per_device, mesh=mesh, in_specs=(spec,) * 10, out_specs=spec, check_vma=False
    )
```
